256 devices in a mesh: occ: 64 (over x, y_lo, z), pair: 4 (over y_hi, core).
Axes of the slice: x: 4, y: 4 (y_hi: 2, y_lo: 2; y = y_hi * 2 + y_lo), z: 8, core: 2. Of those that a mesh axis runs over, the one named last changes fastest.
Arguments:
- three_index: float32 [256, 256, 5120], P(('occ', 'pair')), may hold values from -0.72 to 0.72
- occ_energy: float32 [256], replicated, may hold values from -2 to -0.5
- vir_energy: float32 [256], replicated, may hold values from 0.5 to 4
- coeff: float32 [256, 256], replicated, may hold values from -0.375 to 0.375
- kept: int32 [256, 24], P(('occ', 'pair')), may hold values from 0 to 39, as said below
- owner_slot: int32 [40], replicated, may hold values from 0 to 63, as said below
Outputs:
- pair_energy: float32 [256, 4], P(('occ', 'pair'))
- back_density: bfloat16 [64, 256, 256, 128], P('occ', None, 'pair')
The draws below stay inside these ranges and needn't reach their ends.
Inputs may be any that keep to these rules, and one draw needn't show every extreme that they name: Each row names 24 different blocks; some blocks are kept by far more orbitals than others. `owner_slot`: different blocks have different slots; slot s belongs to owner s.
All inputs are finite; a program needn't handle non-finite values.
Results may differ from the reference program's by a relative error of at most 0.001.
Values sent between devices are 32-bit elements; how exact they have to be, the bound alone decides.
A program may use at most 128 MiB of HBM per device.

```python
import jax
import jax.numpy as jnp
from jax import lax

NVIR = 256
NAUX = 5120
BLOCK = 128
MU = 256
KEEP = 24
NOCC = 256
NBLK = 40
SLOTS = 64
N_OCC = 64
N_PAIR = 4


def draw_kept(key, part):
    popular_key, score_key = jax.random.split(jax.random.fold_in(key, 11))
    popularity = jax.random.randint(popular_key, (NBLK,), 0, 4)
    noise = jax.random.randint(score_key, (NOCC, NBLK), 0, 65536)
    block_ids = jnp.arange(NBLK, dtype=jnp.int32)
    row_ids = jnp.arange(NOCC, dtype=jnp.int32)
    forced = (block_ids[None, :] == (row_ids % NBLK)[:, None]).astype(jnp.int32)
    scores = (noise + popularity[None, :] * 65536 + forced * 8 * 65536) * NBLK + block_ids[None, :]
    values_unused, chosen = lax.top_k(scores, KEEP)
    return chosen.astype(jnp.int32)


def draw_owner_slot(key, part):
    first_key, second_key = jax.random.split(jax.random.fold_in(key, 23))
    remaining = jax.random.permutation(first_key, SLOTS - 1)[:NBLK - 1].astype(jnp.int32)
    chosen = jnp.concatenate([remaining, jnp.array([SLOTS - 1], dtype=jnp.int32)])
    return jax.random.permutation(second_key, chosen).astype(jnp.int32)


def block_levels(stream_key, dims, shards, low, high):
    def one(dim, shards_of):
        steps = jax.random.uniform(jax.random.fold_in(jax.random.fold_in(stream_key, 6), dim), (shards_of,), jnp.float32, low / len(shards), high / len(shards))
        return jnp.repeat(jnp.exp(steps), dims[dim] // shards_of).reshape((-1,) + (1,) * (len(dims) - dim - 1))

    loudness = one(*shards[0])
    for cut in shards[1:]:
        loudness = loudness * one(*cut)
    return loudness


def centred(rng, dims, width, most, shards=(), kind=jnp.bfloat16):
    values = width * jax.random.normal(rng, dims, jnp.float32)
    if shards:
        values = values * block_levels(rng, dims, shards, -0.22, 0.18)
    return jnp.clip(values, -most, most).astype(kind)


def setup_inputs(seed: int = 0) -> dict:
    splits = jax.random.split(jax.random.key(seed), 7)
    three_index = centred(splits[0], (NOCC, NVIR, NAUX), 0.12, 0.72, ((0, 256),), jnp.float32)
    occ_energy = jnp.clip(jax.random.uniform(splits[1], (NOCC,), jnp.float32, -2.0, -0.5), -2.0, -0.5)
    vir_energy = jnp.clip(jax.random.uniform(splits[2], (NVIR,), jnp.float32, 0.5, 4.0), 0.5, 4.0)
    coeff = centred(splits[3], (MU, NOCC), NOCC ** -0.5, 0.375, (), jnp.float32)
    kept = draw_kept(jax.random.fold_in(splits[6], 71), 0)
    owner_slot = draw_owner_slot(jax.random.fold_in(splits[6], 71), 0)
    return {"three_index": three_index, "occ_energy": occ_energy, "vir_energy": vir_energy, "coeff": coeff, "kept": kept, "owner_slot": owner_slot}


def group_terms(group_rows, group_energy, vir_energy):
    pair_count, vir_count, aux_count = group_rows.shape
    rows_total = pair_count * vir_count
    flattened = group_rows.reshape(rows_total, aux_count)
    integrals = jnp.dot(flattened, flattened.T, precision=lax.Precision.HIGHEST).reshape(pair_count, vir_count, pair_count, vir_count)
    denominator = (group_energy[:, None, None, None] + group_energy[None, None, :, None]
                   - vir_energy[None, :, None, None] - vir_energy[None, None, None, :])
    scaled = (2.0 * integrals - jnp.transpose(integrals, (0, 3, 2, 1))) / denominator
    energy_table = jnp.sum(integrals * scaled, axis=(1, 3))
    density = jnp.dot(scaled.reshape(rows_total, rows_total), flattened, precision=lax.Precision.HIGHEST)
    return density.reshape(pair_count, vir_count, aux_count), energy_table


def reference(three_index, occ_energy, vir_energy, coeff, kept, owner_slot):
    grouped = three_index.reshape(N_OCC, N_PAIR, NVIR, NAUX)
    group_energies = occ_energy.reshape(N_OCC, N_PAIR)

    def one_group(group_pack):
        return group_terms(group_pack[0], group_pack[1], vir_energy)

    density_full, energy_tables = lax.map(one_group, (grouped, group_energies))
    pair_energy = energy_tables.reshape(NOCC, N_PAIR)
    density_full = density_full.reshape(NOCC, NVIR, NAUX)
    block_ids = jnp.arange(NBLK, dtype=jnp.int32)

    def one_slot(slot_index):
        matches = owner_slot == slot_index
        block_index = jnp.sum(jnp.where(matches, block_ids, 0)).astype(jnp.int32)
        slot_used = jnp.any(matches)
        live_rows = jnp.logical_and(slot_used, jnp.any(kept == block_index, axis=1))
        weights = coeff * live_rows[None, :].astype(jnp.float32)
        columns = lax.dynamic_slice_in_dim(density_full, (block_index * BLOCK).astype(jnp.int32), BLOCK, 2)
        result = jnp.dot(weights, columns.reshape(NOCC, NVIR * BLOCK), precision=lax.Precision.HIGHEST)
        return result.reshape(MU, NVIR, BLOCK).astype(jnp.bfloat16)

    back_density = lax.map(one_slot, jnp.arange(SLOTS, dtype=jnp.int32))
    return pair_energy, back_density
```

```python
import jax
import jax.numpy as jnp
from jax import lax
from jax.sharding import PartitionSpec as P

BLOCK = 128
PREC = lax.Precision.HIGH


def shards(three_index, occ_energy, vir_energy, coeff, kept, owner_slot):
    pair_count = lax.axis_size("pair")
    occ_count = lax.axis_size("occ")
    group_first = lax.axis_index("occ") * pair_count
    my_place = lax.axis_index("pair")
    group_energy = lax.dynamic_slice_in_dim(occ_energy, group_first, pair_count)
    vir_count = three_index.shape[1]
    aux_count = three_index.shape[2]
    quarter = vir_count // pair_count
    block_count = aux_count // BLOCK
    block_ids = jnp.arange(block_count, dtype=jnp.int32)
    kept_own = jnp.any(kept[0][:, None] == block_ids[None, :], axis=0).astype(jnp.float32)
    live = lax.all_gather(kept_own[None], "pair", axis=0, tiled=True)
    rows = lax.all_gather(three_index, "pair", axis=0, tiled=True)
    mine = lax.dynamic_slice_in_dim(rows, my_place * quarter, quarter, axis=1)
    integrals = jnp.einsum("iap,jbp->iajb", mine, rows, precision=PREC)
    my_vir = lax.dynamic_slice_in_dim(vir_energy, my_place * quarter, quarter)
    denominator = (
        group_energy[:, None, None, None]
        + group_energy[None, None, :, None]
        - my_vir[None, :, None, None]
        - vir_energy[None, None, None, :]
    )
    scaled = (2.0 * integrals - jnp.transpose(integrals, (2, 1, 0, 3))) / denominator
    energies = lax.psum(jnp.sum(integrals * scaled, axis=(1, 3)), "pair")
    pair_energy = lax.dynamic_slice_in_dim(energies, my_place, 1, axis=0)
    density = jnp.einsum("iajb,jbp->iap", scaled, rows, precision=PREC)

    slot_ids = jnp.arange(occ_count, dtype=jnp.int32)
    matches = (owner_slot[None, :] == slot_ids[:, None]).astype(jnp.int32)
    block_of_slot = jnp.sum(matches * block_ids[None, :], axis=1)
    slot_used = jnp.sum(matches, axis=1) > 0
    slot_live = jnp.take(live, block_of_slot, axis=1).T * slot_used[:, None].astype(jnp.float32)
    block_major = density.reshape(pair_count, quarter, block_count, BLOCK).transpose(2, 0, 1, 3)
    outgoing = jnp.take(block_major, block_of_slot, axis=0) * slot_live[:, :, None, None]
    received = lax.all_to_all(outgoing, "occ", split_axis=0, concat_axis=0, tiled=True)
    flattened = received.reshape(coeff.shape[1], quarter, BLOCK)
    result = jnp.einsum("mi,iap->map", coeff, flattened, precision=PREC)
    return (pair_energy, result[None].astype(jnp.bfloat16))


def solution(mesh):
    in_specs = (P(("occ", "pair"), None, None), P(), P(), P(), P(("occ", "pair"), None), P())
    out_specs = (P(("occ", "pair"), None), P("occ", None, "pair", None))
    return jax.shard_map(shards, mesh=mesh, in_specs=in_specs, out_specs=out_specs, check_vma=False)
```

```python
import functools
import numpy as np
import jax
import jax.numpy as jnp
from jax import lax
from jax.experimental import pallas as pl
from jax.experimental.pallas import tpu as pltpu
from jax.sharding import PartitionSpec as P

BLOCK = 128
MESH = pl.DeviceIdType.MESH
NT = (((1,), (1,)), ((), ()))
NN = (((1,), (0,)), ((), ()))


def split(x):
    hi = x.astype(jnp.bfloat16)
    return hi, (x - hi.astype(jnp.float32)).astype(jnp.bfloat16)


def mm(a, b, dims):
    return lax.dot_general(a, b, dims, preferred_element_type=jnp.float32)


def group_kernel(cfg, *refs):
    (xy, ylen, zlen, chunks, wide, caps, unit) = cfg
    refs = list(refs)
    take = lambda n: [refs.pop(0) for _ in range(n)]
    gen, own, vcol, vrow, live = take(5)
    hops = zlen // 2
    if caps:
        stab, rtab = take(2)
        recv, energy_out = take(2)
    else:
        dens, energy_out = take(2)
    ball, rel_n, rel_f, gram, sc, etile, ebuf, lbuf = take(8)
    if caps:
        dens, zsend, xs = take(3)
        arr_p = take(hops)
        arr_m = take(hops)
        zs_p, zr_p, zs_m, zr_m = (take(hops) for _ in range(4))
        xs_s, xs_r, xs_l = take(3)
    loc, s_n, r_n, s_f, r_f, s_fn, b_n, s_ff, b_f, s_o, r_o, s_p, r_p, s_e, r_e, s_l, r_l = take(17)
    occ = lax.axis_index("occ")
    p = lax.axis_index("pair")
    ylo = (occ // zlen) % 2
    flip = occ + zlen - 2 * zlen * ylo
    p_far = (p + 2) % 4
    p_sib = p + 1 - 2 * (p % 2)
    near = (flip, p)
    far = (flip, p_far)
    sib = (occ, p_sib)
    vir = ball.shape[1]
    half = vir // 2
    quarter = vir // 4
    others = [(occ, (p + d) % 4) for d in (1, 2, 3)]
    me = occ // zlen
    z = occ % zlen
    up_z = (occ - z + (z + 1) % zlen, p)
    dn_z = (occ - z + (z + zlen - 1) % zlen, p)

    def cell(d):
        return ((me + d) % xy * zlen + z, p)

    greet = [near, far] + others
    if caps:
        greet = greet + [up_z, dn_z] + [cell(d) for d in range(1, xy)]
    barrier = pltpu.get_barrier_semaphore()
    for dev in greet:
        pl.semaphore_signal(barrier, inc=1, device_id=dev, device_id_type=MESH)
    pl.semaphore_wait(barrier, len(greet))

    def cols(k):
        return pl.ds(pl.multiple_of(k * wide, 128), wide)

    def remote(src, dst, ss, rs, dev):
        return pltpu.make_async_remote_copy(src_ref=src, dst_ref=dst, send_sem=ss, recv_sem=rs,
                                            device_id=dev, device_id_type=MESH)

    lo = pl.ds(0, half)
    up = pl.ds(half, half)

    def c_local(k):
        return pltpu.make_async_copy(own.at[0, :, cols(k)], ball.at[p, :, cols(k)], loc.at[k])

    def c_near(k):
        return remote(ball.at[p, lo, cols(k)], rel_n.at[:, cols(k)], s_n.at[k], r_n.at[k], near)

    def c_far(k):
        return remote(ball.at[p, up, cols(k)], rel_f.at[:, cols(k)], s_f.at[k], r_f.at[k], far)

    def c_fwd_far(k):
        return remote(rel_n.at[:, cols(k)], ball.at[p, lo, cols(k)], s_ff.at[k], b_f.at[k], far)

    def c_fwd_near(k):
        return remote(rel_f.at[:, cols(k)], ball.at[p_far, up, cols(k)], s_fn.at[k], b_n.at[k], near)

    def a_low(k):
        return remote(rel_n.at[:, cols(k)], ball.at[p_far, lo, cols(k)], s_ff.at[k], b_f.at[k], far)

    def a_up(k):
        return remote(rel_f.at[:, cols(k)], ball.at[p_far, up, cols(k)], s_fn.at[k], b_n.at[k], near)

    def c_sib_own(k):
        return remote(ball.at[p, :, cols(k)], ball.at[p, :, cols(k)], s_o.at[k], r_o.at[k], sib)

    def a_sib_own(k):
        return remote(ball.at[p, :, cols(k)], ball.at[p_sib, :, cols(k)], s_o.at[k], r_o.at[k], sib)

    def c_sib_far(k):
        return remote(ball.at[p_far, :, cols(k)], ball.at[p_far, :, cols(k)], s_p.at[k], r_p.at[k], sib)

    p_sibfar = (p_sib + 2) % 4

    def a_sib_far(k):
        return remote(ball.at[p_far, :, cols(k)], ball.at[p_sibfar, :, cols(k)], s_p.at[k], r_p.at[k], sib)

    def loop(n, f):
        lax.fori_loop(0, n, lambda k, c: (f(k), c)[1], 0)

    loop(chunks, lambda k: c_local(k).start())
    lbuf[0] = live[...]

    def c_live(d):
        return remote(live, lbuf.at[d], s_l.at[d - 1], r_l.at[d - 1], (occ, (p + d) % 4))

    def send_own(k):
        c_local(k).wait()
        c_near(k).start()
        c_far(k).start()
        c_sib_own(k).start()

    loop(chunks, send_own)
    for d in (1, 2, 3):
        c_live(d).start()
    gram[...] = jnp.zeros_like(gram)

    def relay(k):
        c_near(k).wait_recv()
        c_fwd_far(k).start()
        c_far(k).wait_recv()
        c_fwd_near(k).start()

    loop(chunks, relay)

    def pass_on(k):
        a_low(k).wait_recv()
        a_up(k).wait_recv()
        c_sib_far(k).start()

    def gram_chunk(k):
        a_sib_own(k).wait_recv()
        a_sib_far(k).wait_recv()
        mine = jnp.concatenate(
            [ball[i, pl.ds(pl.multiple_of(p * quarter, quarter), quarter), cols(k)] for i in range(4)], axis=0)
        hi, low = split(mine)
        both = jnp.concatenate([hi, low], axis=0)
        for j in range(4):
            bh, bl = split(ball[j, :, cols(k)])
            first = mm(both, bh, NT)
            gram[:, j * vir:(j + 1) * vir] += first[:vir] + first[vir:] + mm(hi, bl, NT)

    pass_on(0)

    def step(k):
        pass_on(k + 1)
        gram_chunk(k)

    loop(chunks - 1, step)
    gram_chunk(chunks - 1)

    lane = lax.broadcasted_iota(jnp.int32, (8, 128), 1)
    row = lax.broadcasted_iota(jnp.int32, (8, 128), 0)
    va = vcol[pl.ds(pl.multiple_of(p * quarter, quarter), quarter), :]
    vb = vrow[0:1, :]
    tile = jnp.zeros((8, 128), jnp.float32)
    for i in range(4):
        for j in range(4):
            g = gram[i * quarter:(i + 1) * quarter, j * vir:(j + 1) * vir]
            t = gram[j * quarter:(j + 1) * quarter, i * vir:(i + 1) * vir]
            x = (2.0 * g - t) / (gen[i] + gen[j] - va - vb)
            hi, low = split(x)
            sc[i * quarter:(i + 1) * quarter, j * vir:(j + 1) * vir] = hi
            sc[vir + i * quarter:vir + (i + 1) * quarter, j * vir:(j + 1) * vir] = low
            tile = tile + jnp.where((row == i) & (lane == j), jnp.sum(g * x), 0.0)
    etile[...] = tile

    for d in (1, 2, 3):
        c_live(d).wait()
    live_of = []
    for i in range(4):
        v = jnp.zeros((8, 128), jnp.float32)
        for d in range(4):
            v = v + jnp.where((p + 4 - d) % 4 == i, lbuf[d], 0.0)
        live_of.append(v)

    def c_energy(d):
        return remote(etile, ebuf.at[d - 1], s_e.at[d - 1], r_e.at[d - 1], (occ, (p + d) % 4))

    for d in (1, 2, 3):
        c_energy(d).start()

    def density(k):
        cc = pl.ds(pl.multiple_of(k * 2 * BLOCK, 256), 2 * BLOCK)
        bh, bl = split(ball[:, :, cc].reshape(4 * vir, 2 * BLOCK))
        first = mm(sc[...], bh, NN)
        acc = first[:vir] + first[vir:] + mm(sc[0:vir], bl, NN)
        for h in range(2):
            for i in range(4):
                w = jnp.sum(jnp.where(lane == 2 * k + h, live_of[i], 0.0), axis=1, keepdims=True)[0:1]
                dens[(2 * k + h) * 4 + i] = acc[i * quarter:(i + 1) * quarter, h * BLOCK:(h + 1) * BLOCK] * w

    loop(ball.shape[2] // (2 * BLOCK), density)

    if caps:
        arr = {1: arr_p, -1: arr_m}
        zss = {1: zs_p, -1: zs_m}
        zrs = {1: zr_p, -1: zr_m}
        to = {1: up_z, -1: dn_z}
        side = {1: 0, -1: 1}

        def c_z(sign, h, k):
            src = zsend.at[side[sign]] if h == 0 else arr[sign][h - 1]
            ks = pl.ds(k * unit, unit)
            return remote(src.at[ks], arr[sign][h].at[ks], zss[sign][h].at[k], zrs[sign][h].at[k], to[sign])

        def fill(k):
            for sign in (1, -1):
                for u in range(unit):
                    t = k * unit + u
                    zsend[side[sign], t] = dens[stab[side[sign], t]]

        def send_z(k):
            c_z(1, 0, k).start()
            c_z(-1, 0, k).start()

        fill(0)

        def first_hop(k):
            fill(k + 1)
            send_z(k)

        loop(caps[0] // unit - 1, first_hop)
        send_z(caps[0] // unit - 1)

        nrow = 2 * hops

        def gpos(d):
            return (me + d) % xy

        def c_xy(r, d, zsrc):
            return remote(xs.at[r, gpos(d)], recv.at[me * zlen + zsrc], xs_s.at[r * xy + d],
                          xs_r.at[r * xy + d], cell(d))

        def a_xy(r, d, zsrc):
            return remote(xs.at[r, gpos(d)], recv.at[gpos(xy - d) * zlen + zsrc], xs_s.at[r * xy + d],
                          xs_r.at[r * xy + d], cell(d))

        def c_self(r, zsrc):
            return pltpu.make_async_copy(xs.at[r, me], recv.at[me * zlen + zsrc], xs_l.at[r])

        def place(r, tr, buf, which):
            def one(j):
                for i in which:
                    idx = rtab[tr, j * 4 + i]
                    xs[r, j, i] = jnp.where(idx >= 0, buf[jnp.maximum(idx, 0)], 0.0)
            loop(xy, one)

        def deliver(r, zsrc):
            loop(xy - 1, lambda d: c_xy(r, d + 1, zsrc).start())
            c_self(r, zsrc).start()

        zof = [z]
        place(0, 0, dens, range(4))
        deliver(0, z)
        for h in range(1, hops + 1):
            for sign in (1, -1):
                def forward(k, sign=sign, h=h):
                    c_z(sign, h - 1, k).wait_recv()
                    if h < hops:
                        @pl.when(k < caps[h] // unit)
                        def _():
                            c_z(sign, h, k).start()
                loop(caps[h - 1] // unit, forward)
            if h < hops:
                for sign in (1, -1):
                    r = len(zof)
                    zsrc = (z + zlen - sign * h) % zlen
                    zof.append(zsrc)
                    place(r, h if sign == 1 else hops + h, arr[sign][h - 1], range(4))
                    deliver(r, zsrc)
            else:
                r = len(zof)
                zsrc = (z + h) % zlen
                zof.append(zsrc)
                place(r, h, arr_p[h - 1], (0, 1))
                place(r, hops + h, arr_m[h - 1], (2, 3))
                deliver(r, zsrc)

        for r, zsrc in enumerate(zof):
            c_self(r, zsrc).wait()

            def settle(d, r=r, zsrc=zsrc):
                a_xy(r, d + 1, zsrc).wait_recv()
                c_xy(r, d + 1, zsrc).wait_send()
            loop(xy - 1, settle)
        for h in range(hops):
            for sign in (1, -1):
                loop(caps[h] // unit, lambda k, sign=sign, h=h: c_z(sign, h, k).wait_send())

    for d in (1, 2, 3):
        c_energy(d).wait()
    energy_out[...] = etile[...] + (ebuf[0] + (ebuf[1] + ebuf[2]))

    def drain(k):
        c_near(k).wait_send()
        c_far(k).wait_send()
        c_fwd_far(k).wait_send()
        c_fwd_near(k).wait_send()
        c_sib_own(k).wait_send()
        c_sib_far(k).wait_send()

    loop(chunks, drain)


def group_call(geom, caps, ident, args, tabs):
    three_index = args[1]
    vir, aux = three_index.shape[1], three_index.shape[2]
    xy, ylen, zlen, chunks, unit = geom["xy"], 2, geom["z"], geom["chunks"], geom["unit"]
    wide = aux // chunks
    hops = zlen // 2
    quarter = vir // 4
    dma = lambda *s: pltpu.SemaphoreType.DMA(s)
    f32 = jnp.float32
    vm = pl.BlockSpec(memory_space=pltpu.VMEM)
    sm = pl.BlockSpec(memory_space=pltpu.SMEM)
    hb = pl.BlockSpec(memory_space=pl.ANY)
    piece = (quarter, BLOCK)
    pieces = 4 * aux // BLOCK
    scratch = [
        pltpu.VMEM((4, vir, aux), f32),
        pltpu.VMEM((vir // 2, aux), f32),
        pltpu.VMEM((vir // 2, aux), f32),
        pltpu.VMEM((vir, 4 * vir), f32),
        pltpu.VMEM((2 * vir, 4 * vir), jnp.bfloat16),
        pltpu.VMEM((8, 128), f32),
        pltpu.VMEM((3, 8, 128), f32),
        pltpu.VMEM((4, 8, 128), f32),
    ]
    if caps:
        scratch += [pltpu.VMEM((pieces,) + piece, f32), pltpu.VMEM((2, caps[0]) + piece, f32),
                    pltpu.VMEM((2 * hops, xy, 4) + piece, f32)]
        scratch += [pltpu.VMEM((n,) + piece, f32) for n in caps] * 2
        scratch += [dma(n // unit) for n in caps] * 4
        scratch += [dma(2 * hops * xy), dma(2 * hops * xy), dma(2 * hops)]
    scratch += [dma(chunks)] * 13 + [dma(3)] * 4
    energy = jax.ShapeDtypeStruct((8, 128), f32)
    if caps:
        outs = (jax.ShapeDtypeStruct((xy * zlen, 4) + piece, f32), energy)
    else:
        outs = (jax.ShapeDtypeStruct((pieces,) + piece, f32), energy)
    return pl.pallas_call(
        functools.partial(group_kernel, (xy, ylen, zlen, chunks, wide, caps, unit)),
        out_shape=outs,
        in_specs=[sm, hb, vm, vm, vm] + [sm] * (2 if caps else 0),
        out_specs=(hb if caps else vm, vm),
        scratch_shapes=scratch,
        compiler_params=pltpu.CompilerParams(collective_id=ident, has_side_effects=True,
                                             vmem_limit_bytes=67_000_000),
    )(*args, *(tabs if caps else ()))


def back_kernel(coeff, x, out, tmp):
    chi, clo = split(coeff[...])
    both = jnp.concatenate([chi, clo], axis=0)
    mu = coeff.shape[0]
    rows = x.shape[1]
    for a in range(0, rows, 2):
        xh, xl = split(jnp.concatenate([x[:, a, :], x[:, a + 1, :]], axis=1))
        first = mm(both, xh, NN)
        acc = first[:mu] + first[mu:] + mm(chi, xl, NN)
        tmp[:, a, :] = acc[:, :BLOCK]
        tmp[:, a + 1, :] = acc[:, BLOCK:]
    out[0] = tmp[...].astype(jnp.bfloat16)


def back_call(coeff, x):
    mu, nocc = coeff.shape
    quarter = x.shape[1]
    rows = 16 if quarter % 16 == 0 else quarter
    return pl.pallas_call(
        back_kernel,
        grid=(quarter // rows,),
        out_shape=jax.ShapeDtypeStruct((1, mu, quarter, BLOCK), jnp.bfloat16),
        in_specs=[pl.BlockSpec((mu, nocc), lambda s: (0, 0)),
                  pl.BlockSpec((nocc, rows, BLOCK), lambda s: (0, s, 0))],
        out_specs=pl.BlockSpec((1, mu, rows, BLOCK), lambda s: (0, 0, s, 0)),
        scratch_shapes=[pltpu.VMEM((mu, rows, BLOCK), jnp.float32)],
        compiler_params=pltpu.CompilerParams(vmem_limit_bytes=40 << 20),
    )(coeff, x)


def routes(flags, slot_block, geom, z):
    xy, zlen = geom["xy"], geom["z"]
    hops = zlen // 2
    big = geom["caps"][-1][0]
    src = np.arange(zlen)[:, None]
    dist = np.arange(hops, 0, -1)[None, :]
    stabs, pos, need = [], [], []
    imask = np.ones((2, hops, 4), bool)
    imask[0, 0, 2:] = False
    imask[1, 0, :2] = False
    for s, sign in enumerate((1, -1)):
        dest = (src + sign * dist) % zlen
        f = flags[src, :, dest, :] & imask[s][None, :, None, :]
        flat = f.reshape(zlen, -1).astype(jnp.int32)
        rank = jnp.cumsum(flat, axis=1) - flat
        need.append(jnp.max(jnp.cumsum(jnp.sum(f, axis=(2, 3), dtype=jnp.int32), axis=1)[:, ::-1], axis=0))
        pos.append(jnp.where(f, rank.reshape(f.shape), -1))
        mine_f = lax.dynamic_index_in_dim(flat, z, 0, keepdims=False)
        mine_r = lax.dynamic_index_in_dim(rank, z, 0, keepdims=False)
        block = lax.dynamic_index_in_dim(slot_block.reshape(xy, zlen).T[dest], z, 0, keepdims=False)
        cand = (block[:, :, None] * 4 + jnp.arange(4, dtype=jnp.int32)).reshape(-1)
        hit = (mine_r[None, :] == jnp.arange(big, dtype=jnp.int32)[:, None]) & (mine_f[None, :] > 0)
        stabs.append(jnp.sum(jnp.where(hit, cand[None, :], 0), axis=1))
    own_f = lax.dynamic_index_in_dim(lax.dynamic_index_in_dim(flags, z, 0, keepdims=False), z, 1, keepdims=False)
    own_b = lax.dynamic_index_in_dim(slot_block.reshape(xy, zlen), z, 1, keepdims=False)
    rows = [jnp.where(own_f, own_b[:, None] * 4 + jnp.arange(4, dtype=jnp.int32), -1)]
    for s, sign in enumerate((1, -1)):
        for h in range(1, hops + 1):
            at = (z + zlen - sign * h) % zlen
            rows.append(lax.dynamic_index_in_dim(pos[s][:, hops - h], at, 0, keepdims=False))
    rtab = jnp.stack([r.reshape(-1) for r in rows])
    return jnp.stack(stabs), rtab, jnp.maximum(need[0], need[1])


def shards(geom, three_index, occ_energy, vir_energy, coeff, kept, owner_slot):
    xy, zlen = geom["xy"], geom["z"]
    slots = xy * zlen
    vir, aux = three_index.shape[1], three_index.shape[2]
    block_count = aux // BLOCK
    quarter = vir // 4
    occ = lax.axis_index("occ")
    my_place = lax.axis_index("pair")
    group_energy = lax.dynamic_slice_in_dim(occ_energy, occ * 4, 4)
    block_ids = jnp.arange(block_count, dtype=jnp.int32)
    matches = owner_slot[None, :] == jnp.arange(slots, dtype=jnp.int32)[:, None]
    slot_block = jnp.sum(jnp.where(matches, block_ids[None, :], 0), axis=1)
    used = jnp.any(matches, axis=1)
    kept_here = jnp.any(kept[0][:, None] == block_ids[None, :], axis=0)
    live = jnp.broadcast_to(jnp.pad(kept_here.astype(jnp.float32), (0, 128 - block_count))[None], (8, 128))
    args = (group_energy, three_index, vir_energy.reshape(vir, 1), vir_energy.reshape(1, vir), live)
    flags = jnp.broadcast_to(used.reshape(1, xy, zlen, 1), (zlen, xy, zlen, 4))
    stab, rtab, need = routes(flags, slot_block, geom, occ % zlen)

    def plain(args, stab, rtab):
        dens, tile = group_call(geom, None, 0, args, None)
        picked = jnp.take(dens.reshape(block_count, 4, quarter, BLOCK), slot_block, axis=0)
        out = jnp.where(used[:, None, None, None], picked, 0.0)
        return lax.all_to_all(out, "occ", split_axis=0, concat_axis=0, tiled=True), tile

    branches = [plain]
    fits = jnp.zeros((), jnp.int32)
    for n, caps in enumerate(geom["caps"][::-1]):
        branches.append(lambda args, stab, rtab, caps=caps, n=n: group_call(
            geom, caps, n + 1, args, (stab[:, :caps[0]], rtab)))
        fits = fits + jnp.all(need <= jnp.array(caps, jnp.int32)).astype(jnp.int32)
    recv, tile = lax.switch(fits, branches, args, stab, rtab)
    pair_energy = lax.dynamic_slice(tile, (my_place, 0), (1, 4))
    return (pair_energy, back_call(coeff, recv.reshape(slots * 4, quarter, BLOCK)))


GEOM = {
    64: {"xy": 8, "z": 8, "chunks": 10, "unit": 4,
         "caps": [(76, 56, 36, 12), (84, 64, 40, 16), (92, 72, 44, 16)]},
    4: {"xy": 2, "z": 2, "chunks": 2, "unit": 2, "caps": [(4,), (8,)]},
}


def solution(mesh):
    in_specs = (P(("occ", "pair"), None, None), P(), P(), P(), P(("occ", "pair"), None), P())
    out_specs = (P(("occ", "pair"), None), P("occ", None, "pair", None))
    return jax.shard_map(functools.partial(shards, GEOM[mesh.shape["occ"]]), mesh=mesh, in_specs=in_specs,
                         out_specs=out_specs, check_vma=False)
```

```python
import functools
import jax
import jax.numpy as jnp
from jax import lax
from jax.experimental import pallas as pl
from jax.experimental.pallas import tpu as pltpu
from jax.sharding import PartitionSpec as P

BLOCK = 128
MESH = pl.DeviceIdType.MESH
NT = (((1,), (1,)), ((), ()))
NN = (((1,), (0,)), ((), ()))


def split(x):
    hi = x.astype(jnp.bfloat16)
    return hi, (x - hi.astype(jnp.float32)).astype(jnp.bfloat16)


def mm(a, b, dims):
    return lax.dot_general(a, b, dims, preferred_element_type=jnp.float32)


def group_kernel(cfg, owner, kept, gen, own, vrow,
                 dens_out, energy_out, pos, own_at, stab, level,
                 ball, gram, sc, vcol, dens, etile, ebuf, lbuf, live, row, cells, best, near, rows_s,
                 loc, s_f, r_f, s_o, r_o, s_p, r_p, s_e, r_e, s_l, r_l, s_d, s_c, r_c, s_x, r_x):
    (xy, zlen, chunks, wide, caps, block_count) = cfg
    hops = zlen // 2
    slots = xy * zlen
    occ = lax.axis_index("occ")
    p = lax.axis_index("pair")
    me = occ // zlen
    z = occ % zlen
    p_far = (p + 2) % 4
    p_sib = p + 1 - 2 * (p % 2)
    sib = (occ, p_sib)
    far = (occ, p_far)
    vir = ball.shape[1]
    quarter = vir // 4
    column = [(a, b) for a in range(zlen) for b in range(4) if (a, b) != (0, 0)]

    def mate(a, b):
        return (occ - z + (z + a) % zlen, (p + b) % 4)

    def cell(d):
        return ((me + d) % xy * zlen + z, p)

    def remote(src, dst, ss, rs, dev):
        return pltpu.make_async_remote_copy(src_ref=src, dst_ref=dst, send_sem=ss, recv_sem=rs,
                                            device_id=dev, device_id_type=MESH)

    def loop(n, f):
        lax.fori_loop(0, n, lambda k, c: (f(k), c)[1], 0)

    def cols(k):
        return pl.ds(pl.multiple_of(k * wide, 128), wide)

    def c_local(k):
        return pltpu.make_async_copy(own.at[0, :, cols(k)], ball.at[p, :, cols(k)], loc.at[k])

    barrier = pltpu.get_barrier_semaphore()
    greet = [mate(a, b) for a, b in column] + [cell(d) for d in range(1, xy)]
    for dev in greet:
        pl.semaphore_signal(barrier, inc=1, device_id=dev, device_id_type=MESH)
    loop(chunks, lambda k: c_local(k).start())

    lane = lax.broadcasted_iota(jnp.int32, (8, 128), 1)
    slot = lane % slots
    block = jnp.full((8, 128), -1, jnp.int32)
    for c in range(block_count):
        block = jnp.where(slot == owner[c], c, block)
    have = jnp.zeros((8, 128), jnp.int32)
    alive = jnp.zeros((8, 128), jnp.int32)
    for k in range(kept.shape[1]):
        have = jnp.where(block == kept[0, k], 1, have)
        alive = jnp.where(lane == kept[0, k], 1, alive)
    row[...] = have
    live[...] = alive.astype(jnp.float32)
    lbuf[0] = live[...]
    vcol[...] = jnp.transpose(jnp.broadcast_to(vrow[...], (128, vir)))
    pl.semaphore_wait(barrier, len(greet))

    def c_far(k):
        return remote(ball.at[p, :, cols(k)], ball.at[p, :, cols(k)], s_f.at[k], r_f.at[k], far)

    def a_far(k):
        return remote(ball.at[p, :, cols(k)], ball.at[p_far, :, cols(k)], s_f.at[k], r_f.at[k], far)

    def c_sib_own(k):
        return remote(ball.at[p, :, cols(k)], ball.at[p, :, cols(k)], s_o.at[k], r_o.at[k], sib)

    def a_sib_own(k):
        return remote(ball.at[p, :, cols(k)], ball.at[p_sib, :, cols(k)], s_o.at[k], r_o.at[k], sib)

    def c_sib_far(k):
        return remote(ball.at[p_far, :, cols(k)], ball.at[p_far, :, cols(k)], s_p.at[k], r_p.at[k], sib)

    p_sibfar = (p_sib + 2) % 4

    def a_sib_far(k):
        return remote(ball.at[p_far, :, cols(k)], ball.at[p_sibfar, :, cols(k)], s_p.at[k], r_p.at[k], sib)

    def c_live(d):
        return remote(live, lbuf.at[d], s_l.at[d - 1], r_l.at[d - 1], (occ, (p + d) % 4))

    def c_row(n, a, b):
        return pltpu.make_async_remote_copy(src_ref=row, dst_ref=cells.at[z, p], send_sem=s_c.at[n], recv_sem=r_c.at[a, b],
                                            device_id=mate(a, b), device_id_type=MESH)

    def a_row(n, a, b):
        return pltpu.make_async_remote_copy(src_ref=row, dst_ref=cells.at[(z + zlen - a) % zlen, (p + 4 - b) % 4],
                                            send_sem=s_c.at[n], recv_sem=r_c.at[a, b],
                                            device_id=mate(a, b), device_id_type=MESH)

    def send_own(k):
        c_local(k).wait()
        c_far(k).start()
        c_sib_own(k).start()

    send_own(0)
    for n, (a, b) in enumerate(column):
        c_row(n, a, b).start()
    for d in (1, 2, 3):
        c_live(d).start()
    loop(chunks - 1, lambda k: send_own(k + 1))
    cells[z, p] = row[...]
    gram[...] = jnp.zeros_like(gram)
    for n, (a, b) in enumerate(column):
        a_row(n, a, b).wait_recv()
    source = lax.broadcasted_iota(jnp.int32, (8, 128), 0)
    dest = slot % zlen
    order = slot // zlen
    flag = []
    for i in range(4):
        f = jnp.zeros((8, 128), jnp.int32)
        for a in range(zlen):
            f = jnp.where(source == a, cells[a, i], f)
        flag.append(f)
        own_at[i] = jnp.where(f > 0, block * 4 + i, -1)

    roll = lambda v, n: pltpu.roll(v, n % 128, 1)
    needs = [jnp.zeros((8, 128), jnp.int32) for _ in range(hops)]
    for side, sign in enumerate((1, -1)):
        dist = (sign * (dest - source) + 2 * zlen) % zlen
        xs = []
        for i in range(4):
            tie = (i < 2) == (sign == 1)
            ok = (dist >= 1) & (dist <= (hops if tie else hops - 1))
            xs.append(jnp.where(ok, flag[i], 0))
        totals, before = [], []
        for x in xs:
            t, e, n = x, x, 1
            while n < xy:
                t = t + roll(t, n * zlen)
                e = e + jnp.where(order >= n, roll(e, n * zlen), 0)
                n *= 2
            totals.append(t)
            before.append(e - x)
        total = totals[0] + totals[1] + totals[2] + totals[3]
        farther = jnp.zeros((8, 128), jnp.int32)
        for k in range(1, hops):
            farther = farther + jnp.where(dist + k <= hops, roll(total, -sign * k), 0)
        upto = farther
        for i in range(4):
            pos[side, i] = jnp.where(xs[i] > 0, upto + before[i], -1)
            upto = upto + totals[i]
        for h in range(1, hops + 1):
            needs[h - 1] = jnp.maximum(needs[h - 1], jnp.where(dist == h, farther + total, 0))

    need_tile = jnp.zeros((8, 128), jnp.float32)
    for h in range(hops):
        need_tile = need_tile + jnp.where(lane == h, jnp.max(needs[h].astype(jnp.float32)), 0.0)
    best[...] = need_tile

    at = lax.broadcasted_iota(jnp.int32, (128, 128), 1).astype(jnp.float32)
    inside = lax.broadcasted_iota(jnp.int32, (128, 128), 0) < slots
    tall = lambda v: jnp.transpose(jnp.broadcast_to(v.astype(jnp.float32), (128, 128)))
    rows_s[...] = block
    what = tall(rows_s[0:1, :] * 4)
    for side in range(2):
        acc = jnp.zeros((128, 128), jnp.float32)
        for i in range(4):
            where = tall(pos[side, i, pl.ds(z, 1), :])
            acc = acc + jnp.where((where == at) & inside, what + float(i), 0.0)
        stab[side] = jnp.broadcast_to(jnp.sum(acc, axis=0, keepdims=True), (8, 128)).astype(jnp.int32)


    def c_best(d):
        return remote(best, near.at[d - 1], s_x.at[d - 1], r_x.at[d - 1], cell(d))

    for d in range(1, xy):
        c_best(d).start()

    def pass_on(k):
        a_far(k).wait_recv()
        c_sib_far(k).start()

    def gram_chunk(k):
        a_sib_own(k).wait_recv()
        a_sib_far(k).wait_recv()
        mine = jnp.concatenate(
            [ball[i, pl.ds(pl.multiple_of(p * quarter, quarter), quarter), cols(k)] for i in range(4)], axis=0)
        hi, low = split(mine)
        both = jnp.concatenate([hi, low], axis=0)
        for j in range(4):
            bh, bl = split(ball[j, :, cols(k)])
            first = mm(both, bh, NT)
            gram[:, j * vir:(j + 1) * vir] += first[:vir] + first[vir:] + mm(hi, bl, NT)

    pass_on(0)

    def step(k):
        pass_on(k + 1)
        gram_chunk(k)

    loop(chunks - 1, step)
    gram_chunk(chunks - 1)

    band = lax.broadcasted_iota(jnp.int32, (8, 128), 0)
    va = vcol[pl.ds(pl.multiple_of(p * quarter, quarter), quarter), 0:1]
    vb = vrow[0:1, :]
    tile = jnp.zeros((8, 128), jnp.float32)
    for i in range(4):
        for j in range(4):
            g = gram[i * quarter:(i + 1) * quarter, j * vir:(j + 1) * vir]
            t = gram[j * quarter:(j + 1) * quarter, i * vir:(i + 1) * vir]
            x = (2.0 * g - t) / (gen[occ * 4 + i] + gen[occ * 4 + j] - va - vb)
            hi, low = split(x)
            sc[i * quarter:(i + 1) * quarter, j * vir:(j + 1) * vir] = hi
            sc[vir + i * quarter:vir + (i + 1) * quarter, j * vir:(j + 1) * vir] = low
            tile = tile + jnp.where((band == i) & (lane == j), jnp.sum(g * x), 0.0)
    etile[...] = tile

    for d in (1, 2, 3):
        c_live(d).wait()
    live_of = []
    for i in range(4):
        v = jnp.zeros((8, 128), jnp.float32)
        for d in range(4):
            v = v + jnp.where((p + 4 - d) % 4 == i, lbuf[d], 0.0)
        live_of.append(v)

    def c_energy(d):
        return remote(etile, ebuf.at[d - 1], s_e.at[d - 1], r_e.at[d - 1], (occ, (p + d) % 4))

    for d in (1, 2, 3):
        c_energy(d).start()

    def c_dens(k):
        return pltpu.make_async_copy(dens.at[pl.ds(k * 8, 8)], dens_out.at[pl.ds(k * 8, 8)], s_d.at[k])

    def density(k):
        cc = pl.ds(pl.multiple_of(k * 2 * BLOCK, 256), 2 * BLOCK)
        bh, bl = split(ball[:, :, cc].reshape(4 * vir, 2 * BLOCK))
        first = mm(sc[...], bh, NN)
        acc = first[:vir] + first[vir:] + mm(sc[0:vir], bl, NN)
        for h in range(2):
            for i in range(4):
                w = jnp.sum(jnp.where(lane == 2 * k + h, live_of[i], 0.0), axis=1, keepdims=True)[0:1]
                dens[(2 * k + h) * 4 + i] = acc[i * quarter:(i + 1) * quarter, h * BLOCK:(h + 1) * BLOCK] * w

    steps = block_count // 2
    density(0)

    def dense(k):
        density(k + 1)
        c_dens(k).start()

    loop(steps - 1, dense)

    for d in range(1, xy):
        c_best(d).wait()
    most = best[...]
    for d in range(xy - 1):
        most = jnp.maximum(most, near[d])
    fits = jnp.zeros((8, 128), jnp.int32)
    for cap in caps:
        over = jnp.zeros((8, 128), jnp.float32)
        for h in range(hops):
            over = over + jnp.where((lane == h) & (most > float(cap[h])), 1.0, 0.0)
        fits = fits + jnp.where(jnp.max(over) > 0.0, 0, 1)
    level[...] = fits
    for n, (a, b) in enumerate(column):
        c_row(n, a, b).wait_send()


    c_dens(steps - 1).start()
    for d in (1, 2, 3):
        c_energy(d).wait()
    energy_out[...] = etile[...] + (ebuf[0] + (ebuf[1] + ebuf[2]))

    def drain(k):
        c_far(k).wait_send()
        c_sib_own(k).wait_send()
        c_sib_far(k).wait_send()

    loop(chunks, drain)
    loop(steps, lambda k: c_dens(k).wait())


def group_call(geom, owner_slot, kept, occ_energy, three_index, vir_energy):
    vir, aux = three_index.shape[1], three_index.shape[2]
    xy, zlen, chunks = geom["xy"], geom["z"], geom["chunks"]
    wide = aux // chunks
    quarter = vir // 4
    blocks = aux // BLOCK
    i32, f32 = jnp.int32, jnp.float32
    dma = lambda *s: pltpu.SemaphoreType.DMA(s)
    vm = pl.BlockSpec(memory_space=pltpu.VMEM)
    sm = pl.BlockSpec(memory_space=pltpu.SMEM)
    hb = pl.BlockSpec(memory_space=pl.ANY)
    sd = jax.ShapeDtypeStruct
    tile = (8, 128)
    return pl.pallas_call(
        functools.partial(group_kernel, (xy, zlen, chunks, wide, geom["caps"], blocks)),
        out_shape=(sd((4 * blocks, quarter, BLOCK), f32), sd(tile, f32), sd((2, 4) + tile, i32), sd((4,) + tile, i32),
                   sd((2,) + tile, i32), sd(tile, i32)),
        in_specs=[sm, sm, sm, hb, vm],
        out_specs=(hb, vm, vm, vm, vm, vm),
        scratch_shapes=[
            pltpu.VMEM((4, vir, aux), f32),
            pltpu.VMEM((vir, 4 * vir), f32),
            pltpu.VMEM((2 * vir, 4 * vir), jnp.bfloat16),
            pltpu.VMEM((vir, 128), f32),
            pltpu.VMEM((4 * blocks, quarter, BLOCK), f32),
            pltpu.VMEM(tile, f32),
            pltpu.VMEM((3,) + tile, f32),
            pltpu.VMEM((4,) + tile, f32),
            pltpu.VMEM(tile, f32),
            pltpu.VMEM(tile, i32),
            pltpu.VMEM((zlen, 4) + tile, i32),
            pltpu.VMEM(tile, f32),
            pltpu.VMEM((xy - 1,) + tile, f32),
            pltpu.VMEM(tile, i32),
        ] + [dma(chunks)] * 7 + [dma(3)] * 4 + [dma(blocks // 2), dma(4 * zlen - 1), dma(zlen, 4), dma(xy - 1), dma(xy - 1)],
        compiler_params=pltpu.CompilerParams(collective_id=0, has_side_effects=True, vmem_limit_bytes=58 << 20),
    )(owner_slot, kept, occ_energy, three_index, vir_energy.reshape(1, vir))


def exchange_kernel(cfg, stab, pos, own_at, dens_in, recv, dens, zsend, xs, *refs):
    (xy, zlen, caps, unit) = cfg
    hops = zlen // 2
    rounds = zsend.shape[0]
    rows = zsend.shape[3]
    refs = list(refs)
    take = lambda n: [refs.pop(0) for _ in range(n)]
    keys = [(rd, sign, h) for rd in range(rounds) for sign in (1, -1) for h in range(hops)]
    arr = dict(zip(keys, take(len(keys))))
    zss = dict(zip(keys, take(len(keys))))
    zrs = dict(zip(keys, take(len(keys))))
    xs_s, xs_r, xs_l, s_in = take(4)
    occ = lax.axis_index("occ")
    p = lax.axis_index("pair")
    me = occ // zlen
    z = occ % zlen
    to = {1: (occ - z + (z + 1) % zlen, p), -1: (occ - z + (z + zlen - 1) % zlen, p)}
    side = {1: 0, -1: 1}

    def cell(d):
        return ((me + d) % xy * zlen + z, p)

    def remote(src, dst, ss, rs, dev):
        return pltpu.make_async_remote_copy(src_ref=src, dst_ref=dst, send_sem=ss, recv_sem=rs,
                                            device_id=dev, device_id_type=MESH)

    def loop(n, f):
        lax.fori_loop(0, n, lambda k, c: (f(k), c)[1], 0)

    load = pltpu.make_async_copy(dens_in, dens, s_in)
    load.start()
    greet = [to[1], to[-1]] + [cell(d) for d in range(1, xy)]
    barrier = pltpu.get_barrier_semaphore()
    for dev in greet:
        pl.semaphore_signal(barrier, inc=1, device_id=dev, device_id_type=MESH)
    pl.semaphore_wait(barrier, len(greet))
    load.wait()

    def part(rd):
        return pl.ds(rd * rows, rows)

    def c_z(rd, sign, h, k):
        src = zsend.at[rd, side[sign]] if h == 0 else arr[rd, sign, h - 1]
        ks = pl.ds(k * unit, unit)
        return remote(src.at[ks], arr[rd, sign, h].at[ks], zss[rd, sign, h].at[k], zrs[rd, sign, h].at[k], to[sign])

    def own(rd):
        def fill(k):
            for sign in (1, -1):
                for u in range(unit):
                    t = k * unit + u
                    zsend[rd, side[sign], t] = dens[stab[side[sign], 0, t], part(rd)]

        def send(k):
            c_z(rd, 1, 0, k).start()
            c_z(rd, -1, 0, k).start()

        fill(0)

        def first(k):
            fill(k + 1)
            send(k)

        loop(caps[0] // unit - 1, first)
        send(caps[0] // unit - 1)

    per = 2 * hops

    def gpos(d):
        return (me + d) % xy

    def c_xy(rd, r, d, zsrc):
        n = (rd * per + r) * xy + d
        return remote(xs.at[rd, r, gpos(d)], recv.at[me * zlen + zsrc, :, part(rd)], xs_s.at[n], xs_r.at[n], cell(d))

    def a_xy(rd, r, d, zsrc):
        n = (rd * per + r) * xy + d
        return remote(xs.at[rd, r, gpos(d)], recv.at[gpos(xy - d) * zlen + zsrc, :, part(rd)], xs_s.at[n], xs_r.at[n],
                      cell(d))

    def c_self(rd, r, zsrc):
        return pltpu.make_async_copy(xs.at[rd, r, me], recv.at[me * zlen + zsrc, :, part(rd)], xs_l.at[rd * per + r])

    def place(rd, r, table, buf, which, cut):
        def one(j):
            for i in which:
                idx = table(i, j * zlen + z)
                at = jnp.maximum(idx, 0)
                v = buf[at, part(rd)] if cut else buf[at]
                xs[rd, r, j, i] = jnp.where(idx >= 0, v, 0.0)
        loop(xy, one)

    def stood(sign, zsrc):
        return lambda i, s: pos[side[sign], i, zsrc, s]

    done = []

    def deliver(rd, r, zsrc):
        loop(xy - 1, lambda d: c_xy(rd, r, d + 1, zsrc).start())
        c_self(rd, r, zsrc).start()
        done.append((rd, r, zsrc))

    def hop(rd, h):
        for sign in (1, -1):
            def forward(k, sign=sign):
                c_z(rd, sign, h - 1, k).wait_recv()
                if h < hops:
                    @pl.when(k < caps[h] // unit)
                    def _():
                        c_z(rd, sign, h, k).start()
            loop(caps[h - 1] // unit, forward)

    def settle(rd, h):
        if h < hops:
            for n, sign in enumerate((1, -1)):
                r = 1 + 2 * (h - 1) + n
                zsrc = (z + zlen - sign * h) % zlen
                place(rd, r, stood(sign, zsrc), arr[rd, sign, h - 1], range(4), False)
                deliver(rd, r, zsrc)
        else:
            r = 2 * hops - 1
            zsrc = (z + h) % zlen
            place(rd, r, stood(1, zsrc), arr[rd, 1, h - 1], (0, 1), False)
            place(rd, r, stood(-1, zsrc), arr[rd, -1, h - 1], (2, 3), False)
            deliver(rd, r, zsrc)

    own(0)
    for rd in range(rounds):
        place(rd, 0, lambda i, s: own_at[i, z, s], dens, range(4), True)
        deliver(rd, 0, z)
    hop(0, 1)
    settle(0, 1)
    hop(0, 2)
    own(1)
    settle(0, 2)
    hop(0, 3)
    settle(0, 3)
    hop(1, 1)
    hop(0, 4)
    settle(0, 4)
    settle(1, 1)
    for h in (2, 3, 4):
        hop(1, h)
        settle(1, h)

    for rd, r, zsrc in done:
        c_self(rd, r, zsrc).wait()

        def finish(d, rd=rd, r=r, zsrc=zsrc):
            a_xy(rd, r, d + 1, zsrc).wait_recv()
            c_xy(rd, r, d + 1, zsrc).wait_send()
        loop(xy - 1, finish)
    for rd, sign, h in keys:
        loop(caps[h] // unit, lambda k, rd=rd, sign=sign, h=h: c_z(rd, sign, h, k).wait_send())


def exchange_call(geom, caps, ident, dens, stab, pos, own_at):
    xy, zlen, unit = geom["xy"], geom["z"], geom["unit"]
    hops = zlen // 2
    rounds = 2
    quarter = dens.shape[1]
    rows = quarter // rounds
    f32 = jnp.float32
    dma = lambda *s: pltpu.SemaphoreType.DMA(s)
    sm = pl.BlockSpec(memory_space=pltpu.SMEM)
    hb = pl.BlockSpec(memory_space=pl.ANY)
    piece = (rows, BLOCK)
    order = [caps[h] for rd in range(rounds) for sign in (1, -1) for h in range(hops)]
    n = rounds * 2 * hops
    return pl.pallas_call(
        functools.partial(exchange_kernel, (xy, zlen, caps, unit)),
        out_shape=jax.ShapeDtypeStruct((xy * zlen, 4, quarter, BLOCK), f32),
        in_specs=[sm, sm, sm, hb],
        out_specs=hb,
        scratch_shapes=[pltpu.VMEM(dens.shape, f32), pltpu.VMEM((rounds, 2, caps[0]) + piece, f32),
                        pltpu.VMEM((rounds, 2 * hops, xy, 4) + piece, f32)]
        + [pltpu.VMEM((c,) + piece, f32) for c in order] + [dma(c // unit) for c in order] * 2
        + [dma(n * xy), dma(n * xy), dma(n), pltpu.SemaphoreType.DMA],
        compiler_params=pltpu.CompilerParams(collective_id=ident, has_side_effects=True, vmem_limit_bytes=58 << 20),
    )(stab, pos, own_at, dens)


def back_kernel(coeff, x, out, tmp):
    chi, clo = split(coeff[...])
    both = jnp.concatenate([chi, clo], axis=0)
    mu = coeff.shape[0]
    rows = x.shape[1]
    for a in range(0, rows, 2):
        xh, xl = split(jnp.concatenate([x[:, a, :], x[:, a + 1, :]], axis=1))
        first = mm(both, xh, NN)
        acc = first[:mu] + first[mu:] + mm(chi, xl, NN)
        tmp[:, a, :] = acc[:, :BLOCK]
        tmp[:, a + 1, :] = acc[:, BLOCK:]
    out[0] = tmp[...].astype(jnp.bfloat16)


def back_call(coeff, x):
    mu, nocc = coeff.shape
    quarter = x.shape[1]
    rows = 16 if quarter % 16 == 0 else quarter
    return pl.pallas_call(
        back_kernel,
        grid=(quarter // rows,),
        out_shape=jax.ShapeDtypeStruct((1, mu, quarter, BLOCK), jnp.bfloat16),
        in_specs=[pl.BlockSpec((mu, nocc), lambda s: (0, 0)),
                  pl.BlockSpec((nocc, rows, BLOCK), lambda s: (0, s, 0))],
        out_specs=pl.BlockSpec((1, mu, rows, BLOCK), lambda s: (0, 0, s, 0)),
        scratch_shapes=[pltpu.VMEM((mu, rows, BLOCK), jnp.float32)],
        compiler_params=pltpu.CompilerParams(vmem_limit_bytes=40 << 20),
    )(coeff, x)


def shards(geom, three_index, occ_energy, vir_energy, coeff, kept, owner_slot):
    xy, zlen = geom["xy"], geom["z"]
    slots = xy * zlen
    vir, aux = three_index.shape[1], three_index.shape[2]
    block_count = aux // BLOCK
    quarter = vir // 4
    my_place = lax.axis_index("pair")
    dens, tile, pos, own_at, stab, level = group_call(geom, owner_slot, kept, occ_energy, three_index, vir_energy)

    def plain(dens, stab, pos, own_at, owner_slot):
        matches = owner_slot[None, :] == jnp.arange(slots, dtype=jnp.int32)[:, None]
        slot_block = jnp.sum(jnp.where(matches, jnp.arange(block_count, dtype=jnp.int32)[None, :], 0), axis=1)
        used = jnp.any(matches, axis=1)
        picked = jnp.take(dens.reshape(block_count, 4, quarter, BLOCK), slot_block, axis=0)
        out = jnp.where(used[:, None, None, None], picked, 0.0)
        return lax.all_to_all(out, "occ", split_axis=0, concat_axis=0, tiled=True)

    branches = [plain]
    for n, caps in enumerate(geom["caps"][::-1]):
        branches.append(lambda dens, stab, pos, own_at, owner_slot, caps=caps, n=n: exchange_call(
            geom, caps, n + 1, dens, stab, pos, own_at))
    recv = lax.switch(level[0, 0], branches, dens, stab, pos, own_at, owner_slot)
    pair_energy = lax.dynamic_slice(tile, (my_place, 0), (1, 4))
    return (pair_energy, back_call(coeff, recv.reshape(slots * 4, quarter, BLOCK)))


GEOM = {
    64: {"xy": 8, "z": 8, "chunks": 10, "unit": 4,
         "caps": [(52, 40, 28, 12), (56, 44, 28, 12), (60, 48, 32, 16), (68, 56, 36, 16), (80, 64, 44, 16)]},
}


def solution(mesh):
    in_specs = (P(("occ", "pair"), None, None), P(), P(), P(), P(("occ", "pair"), None), P())
    out_specs = (P(("occ", "pair"), None), P("occ", None, "pair", None))
    return jax.shard_map(functools.partial(shards, GEOM[mesh.shape["occ"]]), mesh=mesh, in_specs=in_specs,
                         out_specs=out_specs, check_vma=False)
```

```python
import functools
import jax
import jax.numpy as jnp
from jax import lax
from jax.experimental import pallas as pl
from jax.experimental.pallas import tpu as pltpu
from jax.sharding import PartitionSpec as P

BLOCK = 128
MESH = pl.DeviceIdType.MESH
NT = (((1,), (1,)), ((), ()))
NN = (((1,), (0,)), ((), ()))


def split(x):
    hi = x.astype(jnp.bfloat16)
    return hi, (x - hi.astype(jnp.float32)).astype(jnp.bfloat16)


def mm(a, b, dims):
    return lax.dot_general(a, b, dims, preferred_element_type=jnp.float32)


def group_kernel(cfg, owner, kept, gen, own, vrow,
                 dens_out, energy_out, pos, own_at, stab, level,
                 ball, gram, sc, vcol, dens, etile, ebuf, lbuf, live, row, cells, best, near, rows_s,
                 loc, s_f, r_f, s_o, r_o, s_p, r_p, s_e, r_e, s_l, r_l, s_d, s_c, r_c, s_x, r_x):
    (xy, zlen, chunks, wide, caps, block_count) = cfg
    hops = zlen // 2
    slots = xy * zlen
    occ = lax.axis_index("occ")
    p = lax.axis_index("pair")
    me = occ // zlen
    z = occ % zlen
    p_far = (p + 2) % 4
    p_sib = p + 1 - 2 * (p % 2)
    sib = (occ, p_sib)
    far = (occ, p_far)
    vir = ball.shape[1]
    quarter = vir // 4
    column = [(a, b) for a in range(zlen) for b in range(4) if (a, b) != (0, 0)]

    def mate(a, b):
        return (occ - z + (z + a) % zlen, (p + b) % 4)

    def cell(d):
        return ((me + d) % xy * zlen + z, p)

    def remote(src, dst, ss, rs, dev):
        return pltpu.make_async_remote_copy(src_ref=src, dst_ref=dst, send_sem=ss, recv_sem=rs,
                                            device_id=dev, device_id_type=MESH)

    def loop(n, f):
        lax.fori_loop(0, n, lambda k, c: (f(k), c)[1], 0)

    def cols(k):
        return pl.ds(pl.multiple_of(k * wide, 128), wide)

    def c_local(k):
        return pltpu.make_async_copy(own.at[0, :, cols(k)], ball.at[p, :, cols(k)], loc.at[k])

    barrier = pltpu.get_barrier_semaphore()
    greet = [mate(a, b) for a, b in column] + [cell(d) for d in range(1, xy)]
    for dev in greet:
        pl.semaphore_signal(barrier, inc=1, device_id=dev, device_id_type=MESH)
    loop(chunks, lambda k: c_local(k).start())

    lane = lax.broadcasted_iota(jnp.int32, (8, 128), 1)
    slot = lane % slots
    block = jnp.full((8, 128), -1, jnp.int32)
    for c in range(block_count):
        block = jnp.where(slot == owner[c], c, block)
    have = jnp.zeros((8, 128), jnp.int32)
    alive = jnp.zeros((8, 128), jnp.int32)
    for k in range(kept.shape[1]):
        have = jnp.where(block == kept[0, k], 1, have)
        alive = jnp.where(lane == kept[0, k], 1, alive)
    row[...] = have
    live[...] = alive.astype(jnp.float32)
    lbuf[0] = live[...]
    vcol[...] = jnp.transpose(jnp.broadcast_to(vrow[...], (128, vir)))
    pl.semaphore_wait(barrier, len(greet))

    def c_far(k):
        return remote(ball.at[p, :, cols(k)], ball.at[p, :, cols(k)], s_f.at[k], r_f.at[k], far)

    def a_far(k):
        return remote(ball.at[p, :, cols(k)], ball.at[p_far, :, cols(k)], s_f.at[k], r_f.at[k], far)

    def c_sib_own(k):
        return remote(ball.at[p, :, cols(k)], ball.at[p, :, cols(k)], s_o.at[k], r_o.at[k], sib)

    def a_sib_own(k):
        return remote(ball.at[p, :, cols(k)], ball.at[p_sib, :, cols(k)], s_o.at[k], r_o.at[k], sib)

    def c_sib_far(k):
        return remote(ball.at[p_far, :, cols(k)], ball.at[p_far, :, cols(k)], s_p.at[k], r_p.at[k], sib)

    p_sibfar = (p_sib + 2) % 4

    def a_sib_far(k):
        return remote(ball.at[p_far, :, cols(k)], ball.at[p_sibfar, :, cols(k)], s_p.at[k], r_p.at[k], sib)

    def c_live(d):
        return remote(live, lbuf.at[d], s_l.at[d - 1], r_l.at[d - 1], (occ, (p + d) % 4))

    def c_row(n, a, b):
        return pltpu.make_async_remote_copy(src_ref=row, dst_ref=cells.at[z, p], send_sem=s_c.at[n], recv_sem=r_c.at[a, b],
                                            device_id=mate(a, b), device_id_type=MESH)

    def a_row(n, a, b):
        return pltpu.make_async_remote_copy(src_ref=row, dst_ref=cells.at[(z + zlen - a) % zlen, (p + 4 - b) % 4],
                                            send_sem=s_c.at[n], recv_sem=r_c.at[a, b],
                                            device_id=mate(a, b), device_id_type=MESH)

    def send_own(k):
        c_local(k).wait()
        c_far(k).start()
        c_sib_own(k).start()

    send_own(0)
    for n, (a, b) in enumerate(column):
        c_row(n, a, b).start()
    for d in (1, 2, 3):
        c_live(d).start()
    loop(chunks - 1, lambda k: send_own(k + 1))
    cells[z, p] = row[...]
    gram[...] = jnp.zeros_like(gram)
    for n, (a, b) in enumerate(column):
        a_row(n, a, b).wait_recv()
    source = lax.broadcasted_iota(jnp.int32, (8, 128), 0)
    dest = slot % zlen
    order = slot // zlen
    flag = []
    for i in range(4):
        f = jnp.zeros((8, 128), jnp.int32)
        for a in range(zlen):
            f = jnp.where(source == a, cells[a, i], f)
        flag.append(f)
        own_at[i] = jnp.where(f > 0, block * 4 + i, -1)

    roll = lambda v, n: pltpu.roll(v, n % 128, 1)
    needs = [jnp.zeros((8, 128), jnp.int32) for _ in range(hops)]
    for side, sign in enumerate((1, -1)):
        dist = (sign * (dest - source) + 2 * zlen) % zlen
        xs = []
        for i in range(4):
            tie = (i < 2) == (sign == 1)
            ok = (dist >= 1) & (dist <= (hops if tie else hops - 1))
            xs.append(jnp.where(ok, flag[i], 0))
        totals, before = [], []
        for x in xs:
            t, e, n = x, x, 1
            while n < xy:
                t = t + roll(t, n * zlen)
                e = e + jnp.where(order >= n, roll(e, n * zlen), 0)
                n *= 2
            totals.append(t)
            before.append(e - x)
        total = totals[0] + totals[1] + totals[2] + totals[3]
        farther = jnp.zeros((8, 128), jnp.int32)
        for k in range(1, hops):
            farther = farther + jnp.where(dist + k <= hops, roll(total, -sign * k), 0)
        upto = farther
        for i in range(4):
            pos[side, i] = jnp.where(xs[i] > 0, upto + before[i], -1)
            upto = upto + totals[i]
        for h in range(1, hops + 1):
            needs[h - 1] = jnp.maximum(needs[h - 1], jnp.where(dist == h, farther + total, 0))

    need_tile = jnp.zeros((8, 128), jnp.float32)
    for h in range(hops):
        need_tile = need_tile + jnp.where(lane == h, jnp.max(needs[h].astype(jnp.float32)), 0.0)
    best[...] = need_tile

    at = lax.broadcasted_iota(jnp.int32, (128, 128), 1).astype(jnp.float32)
    inside = lax.broadcasted_iota(jnp.int32, (128, 128), 0) < slots
    tall = lambda v: jnp.transpose(jnp.broadcast_to(v.astype(jnp.float32), (128, 128)))
    rows_s[...] = block
    what = tall(rows_s[0:1, :] * 4)
    for side in range(2):
        acc = jnp.zeros((128, 128), jnp.float32)
        for i in range(4):
            where = tall(pos[side, i, pl.ds(z, 1), :])
            acc = acc + jnp.where((where == at) & inside, what + float(i), 0.0)
        stab[side] = jnp.broadcast_to(jnp.sum(acc, axis=0, keepdims=True), (8, 128)).astype(jnp.int32)


    def c_best(d):
        return remote(best, near.at[d - 1], s_x.at[d - 1], r_x.at[d - 1], cell(d))

    for d in range(1, xy):
        c_best(d).start()

    def pass_on(k):
        a_far(k).wait_recv()
        c_sib_far(k).start()

    def gram_chunk(k):
        a_sib_own(k).wait_recv()
        a_sib_far(k).wait_recv()
        mine = jnp.concatenate(
            [ball[i, pl.ds(pl.multiple_of(p * quarter, quarter), quarter), cols(k)] for i in range(4)], axis=0)
        hi, low = split(mine)
        both = jnp.concatenate([hi, low], axis=0)
        for j in range(4):
            bh, bl = split(ball[j, :, cols(k)])
            first = mm(both, bh, NT)
            gram[:, j * vir:(j + 1) * vir] += first[:vir] + first[vir:] + mm(hi, bl, NT)

    pass_on(0)

    def step(k):
        pass_on(k + 1)
        gram_chunk(k)

    loop(chunks - 1, step)
    gram_chunk(chunks - 1)

    band = lax.broadcasted_iota(jnp.int32, (8, 128), 0)
    va = vcol[pl.ds(pl.multiple_of(p * quarter, quarter), quarter), 0:1]
    vb = vrow[0:1, :]
    tile = jnp.zeros((8, 128), jnp.float32)
    for i in range(4):
        for j in range(4):
            g = gram[i * quarter:(i + 1) * quarter, j * vir:(j + 1) * vir]
            t = gram[j * quarter:(j + 1) * quarter, i * vir:(i + 1) * vir]
            x = (2.0 * g - t) / (gen[occ * 4 + i] + gen[occ * 4 + j] - va - vb)
            hi, low = split(x)
            sc[i * quarter:(i + 1) * quarter, j * vir:(j + 1) * vir] = hi
            sc[vir + i * quarter:vir + (i + 1) * quarter, j * vir:(j + 1) * vir] = low
            tile = tile + jnp.where((band == i) & (lane == j), jnp.sum(g * x), 0.0)
    etile[...] = tile

    for d in (1, 2, 3):
        c_live(d).wait()
    live_of = []
    for i in range(4):
        v = jnp.zeros((8, 128), jnp.float32)
        for d in range(4):
            v = v + jnp.where((p + 4 - d) % 4 == i, lbuf[d], 0.0)
        live_of.append(v)

    def c_energy(d):
        return remote(etile, ebuf.at[d - 1], s_e.at[d - 1], r_e.at[d - 1], (occ, (p + d) % 4))

    for d in (1, 2, 3):
        c_energy(d).start()

    def c_dens(k):
        return pltpu.make_async_copy(dens.at[pl.ds(k * 8, 8)], dens_out.at[pl.ds(k * 8, 8)], s_d.at[k])

    def density(k):
        cc = pl.ds(pl.multiple_of(k * 2 * BLOCK, 256), 2 * BLOCK)
        bh, bl = split(ball[:, :, cc].reshape(4 * vir, 2 * BLOCK))
        first = mm(sc[...], bh, NN)
        acc = first[:vir] + first[vir:] + mm(sc[0:vir], bl, NN)
        for h in range(2):
            for i in range(4):
                w = jnp.sum(jnp.where(lane == 2 * k + h, live_of[i], 0.0), axis=1, keepdims=True)[0:1]
                dens[(2 * k + h) * 4 + i] = acc[i * quarter:(i + 1) * quarter, h * BLOCK:(h + 1) * BLOCK] * w

    steps = block_count // 2
    density(0)

    def dense(k):
        density(k + 1)
        c_dens(k).start()

    loop(steps - 1, dense)

    for d in range(1, xy):
        c_best(d).wait()
    most = best[...]
    for d in range(xy - 1):
        most = jnp.maximum(most, near[d])
    fits = jnp.zeros((8, 128), jnp.int32)
    for cap in caps:
        over = jnp.zeros((8, 128), jnp.float32)
        for h in range(hops):
            over = over + jnp.where((lane == h) & (most > float(cap[h])), 1.0, 0.0)
        fits = fits + jnp.where(jnp.max(over) > 0.0, 0, 1)
    level[...] = fits
    for n, (a, b) in enumerate(column):
        c_row(n, a, b).wait_send()


    c_dens(steps - 1).start()
    for d in (1, 2, 3):
        c_energy(d).wait()
    etile[...] = etile[...] + (ebuf[0] + (ebuf[1] + ebuf[2]))
    energy_out[...] = etile[pl.ds(p, 1), 0:4]

    def drain(k):
        c_far(k).wait_send()
        c_sib_own(k).wait_send()
        c_sib_far(k).wait_send()

    loop(chunks, drain)
    loop(steps, lambda k: c_dens(k).wait())


def group_call(geom, owner_slot, kept, occ_energy, three_index, vir_energy):
    vir, aux = three_index.shape[1], three_index.shape[2]
    xy, zlen, chunks = geom["xy"], geom["z"], geom["chunks"]
    wide = aux // chunks
    quarter = vir // 4
    blocks = aux // BLOCK
    i32, f32 = jnp.int32, jnp.float32
    dma = lambda *s: pltpu.SemaphoreType.DMA(s)
    vm = pl.BlockSpec(memory_space=pltpu.VMEM)
    sm = pl.BlockSpec(memory_space=pltpu.SMEM)
    hb = pl.BlockSpec(memory_space=pl.ANY)
    sd = jax.ShapeDtypeStruct
    tile = (8, 128)
    return pl.pallas_call(
        functools.partial(group_kernel, (xy, zlen, chunks, wide, geom["caps"], blocks)),
        out_shape=(sd((4 * blocks, quarter, BLOCK), f32), sd((1, 4), f32), sd((2, 4) + tile, i32), sd((4,) + tile, i32),
                   sd((2,) + tile, i32), sd(tile, i32)),
        in_specs=[sm, sm, sm, hb, vm],
        out_specs=(hb, vm, vm, vm, vm, vm),
        scratch_shapes=[
            pltpu.VMEM((4, vir, aux), f32),
            pltpu.VMEM((vir, 4 * vir), f32),
            pltpu.VMEM((2 * vir, 4 * vir), jnp.bfloat16),
            pltpu.VMEM((vir, 128), f32),
            pltpu.VMEM((4 * blocks, quarter, BLOCK), f32),
            pltpu.VMEM(tile, f32),
            pltpu.VMEM((3,) + tile, f32),
            pltpu.VMEM((4,) + tile, f32),
            pltpu.VMEM(tile, f32),
            pltpu.VMEM(tile, i32),
            pltpu.VMEM((zlen, 4) + tile, i32),
            pltpu.VMEM(tile, f32),
            pltpu.VMEM((xy - 1,) + tile, f32),
            pltpu.VMEM(tile, i32),
        ] + [dma(chunks)] * 7 + [dma(3)] * 4 + [dma(blocks // 2), dma(4 * zlen - 1), dma(zlen, 4), dma(xy - 1), dma(xy - 1)],
        compiler_params=pltpu.CompilerParams(collective_id=0, has_side_effects=True, vmem_limit_bytes=58 << 20),
    )(owner_slot, kept, occ_energy, three_index, vir_energy.reshape(1, vir))


def exchange_kernel(cfg, stab, pos, own_at, dens_in, recv, dens, zsend, xs, *refs):
    (xy, zlen, caps, unit) = cfg
    hops = zlen // 2
    rounds = zsend.shape[0]
    rows = zsend.shape[3]
    refs = list(refs)
    take = lambda n: [refs.pop(0) for _ in range(n)]
    keys = [(rd, sign, h) for rd in range(rounds) for sign in (1, -1) for h in range(hops)]
    arr = dict(zip(keys, take(len(keys))))
    zss = dict(zip(keys, take(len(keys))))
    zrs = dict(zip(keys, take(len(keys))))
    xs_s, xs_r, xs_l, s_in = take(4)
    occ = lax.axis_index("occ")
    p = lax.axis_index("pair")
    me = occ // zlen
    z = occ % zlen
    to = {1: (occ - z + (z + 1) % zlen, p), -1: (occ - z + (z + zlen - 1) % zlen, p)}
    side = {1: 0, -1: 1}

    def cell(d):
        return ((me + d) % xy * zlen + z, p)

    def remote(src, dst, ss, rs, dev):
        return pltpu.make_async_remote_copy(src_ref=src, dst_ref=dst, send_sem=ss, recv_sem=rs,
                                            device_id=dev, device_id_type=MESH)

    def loop(n, f):
        lax.fori_loop(0, n, lambda k, c: (f(k), c)[1], 0)

    load = pltpu.make_async_copy(dens_in, dens, s_in)
    load.start()
    greet = [to[1], to[-1]] + [cell(d) for d in range(1, xy)]
    barrier = pltpu.get_barrier_semaphore()
    for dev in greet:
        pl.semaphore_signal(barrier, inc=1, device_id=dev, device_id_type=MESH)
    pl.semaphore_wait(barrier, len(greet))
    load.wait()

    def part(rd):
        return pl.ds(rd * rows, rows)

    def c_z(rd, sign, h, k):
        src = zsend.at[rd, side[sign]] if h == 0 else arr[rd, sign, h - 1]
        ks = pl.ds(k * unit, unit)
        return remote(src.at[ks], arr[rd, sign, h].at[ks], zss[rd, sign, h].at[k], zrs[rd, sign, h].at[k], to[sign])

    def own(rd):
        def fill(k):
            for sign in (1, -1):
                for u in range(unit):
                    t = k * unit + u
                    zsend[rd, side[sign], t] = dens[stab[side[sign], 0, t], part(rd)]

        def send(k):
            c_z(rd, 1, 0, k).start()
            c_z(rd, -1, 0, k).start()

        fill(0)

        def first(k):
            fill(k + 1)
            send(k)

        loop(caps[0] // unit - 1, first)
        send(caps[0] // unit - 1)

    per = 2 * hops

    def gpos(d):
        return (me + d) % xy

    def c_xy(rd, r, d, zsrc):
        n = (rd * per + r) * xy + d
        return remote(xs.at[rd, r, gpos(d)], recv.at[me * zlen + zsrc, :, part(rd)], xs_s.at[n], xs_r.at[n], cell(d))

    def a_xy(rd, r, d, zsrc):
        n = (rd * per + r) * xy + d
        return remote(xs.at[rd, r, gpos(d)], recv.at[gpos(xy - d) * zlen + zsrc, :, part(rd)], xs_s.at[n], xs_r.at[n],
                      cell(d))

    def c_self(rd, r, zsrc):
        return pltpu.make_async_copy(xs.at[rd, r, me], recv.at[me * zlen + zsrc, :, part(rd)], xs_l.at[rd * per + r])

    def place(rd, r, table, buf, which, cut):
        def one(j):
            for i in which:
                idx = table(i, j * zlen + z)
                at = jnp.maximum(idx, 0)
                v = buf[at, part(rd)] if cut else buf[at]
                xs[rd, r, j, i] = jnp.where(idx >= 0, v, 0.0)
        loop(xy, one)

    def stood(sign, zsrc):
        return lambda i, s: pos[side[sign], i, zsrc, s]

    done = []

    def deliver(rd, r, zsrc):
        loop(xy - 1, lambda d: c_xy(rd, r, d + 1, zsrc).start())
        c_self(rd, r, zsrc).start()
        done.append((rd, r, zsrc))

    def hop(rd, h):
        def forward(k):
            for sign in (1, -1):
                c_z(rd, sign, h - 1, k).wait_recv()
                if h < hops:
                    @pl.when(k < caps[h] // unit)
                    def _(sign=sign):
                        c_z(rd, sign, h, k).start()
        loop(caps[h - 1] // unit, forward)

    def settle(rd, h):
        if h < hops:
            for n, sign in enumerate((1, -1)):
                r = 1 + 2 * (h - 1) + n
                zsrc = (z + zlen - sign * h) % zlen
                place(rd, r, stood(sign, zsrc), arr[rd, sign, h - 1], range(4), False)
                deliver(rd, r, zsrc)
        else:
            r = 2 * hops - 1
            zsrc = (z + h) % zlen
            place(rd, r, stood(1, zsrc), arr[rd, 1, h - 1], (0, 1), False)
            place(rd, r, stood(-1, zsrc), arr[rd, -1, h - 1], (2, 3), False)
            deliver(rd, r, zsrc)

    own(0)
    for rd in range(rounds):
        place(rd, 0, lambda i, s: own_at[i, z, s], dens, range(4), True)
        deliver(rd, 0, z)
    hop(0, 1)
    settle(0, 1)
    hop(0, 2)
    own(1)
    settle(0, 2)
    hop(0, 3)
    settle(0, 3)
    hop(1, 1)
    hop(0, 4)
    settle(0, 4)
    settle(1, 1)
    for h in (2, 3, 4):
        hop(1, h)
        settle(1, h)

    for rd, r, zsrc in done:
        c_self(rd, r, zsrc).wait()

        def finish(d, rd=rd, r=r, zsrc=zsrc):
            a_xy(rd, r, d + 1, zsrc).wait_recv()
            c_xy(rd, r, d + 1, zsrc).wait_send()
        loop(xy - 1, finish)
    for rd, sign, h in keys:
        loop(caps[h] // unit, lambda k, rd=rd, sign=sign, h=h: c_z(rd, sign, h, k).wait_send())


def exchange_call(geom, caps, ident, dens, stab, pos, own_at):
    xy, zlen, unit = geom["xy"], geom["z"], geom["unit"]
    hops = zlen // 2
    rounds = 2
    quarter = dens.shape[1]
    rows = quarter // rounds
    f32 = jnp.float32
    dma = lambda *s: pltpu.SemaphoreType.DMA(s)
    sm = pl.BlockSpec(memory_space=pltpu.SMEM)
    hb = pl.BlockSpec(memory_space=pl.ANY)
    piece = (rows, BLOCK)
    order = [caps[h] for rd in range(rounds) for sign in (1, -1) for h in range(hops)]
    n = rounds * 2 * hops
    return pl.pallas_call(
        functools.partial(exchange_kernel, (xy, zlen, caps, unit)),
        out_shape=jax.ShapeDtypeStruct((xy * zlen, 4, quarter, BLOCK), f32),
        in_specs=[sm, sm, sm, hb],
        out_specs=hb,
        scratch_shapes=[pltpu.VMEM(dens.shape, f32), pltpu.VMEM((rounds, 2, caps[0]) + piece, f32),
                        pltpu.VMEM((rounds, 2 * hops, xy, 4) + piece, f32)]
        + [pltpu.VMEM((c,) + piece, f32) for c in order] + [dma(c // unit) for c in order] * 2
        + [dma(n * xy), dma(n * xy), dma(n), pltpu.SemaphoreType.DMA],
        compiler_params=pltpu.CompilerParams(collective_id=ident, has_side_effects=True, vmem_limit_bytes=58 << 20),
    )(stab, pos, own_at, dens)


def back_kernel(coeff, x, out, tmp):
    chi, clo = split(coeff[...])
    both = jnp.concatenate([chi, clo], axis=0)
    mu = coeff.shape[0]
    rows = x.shape[1]
    turned = jnp.transpose(x[...], (1, 0, 2))
    for a in range(0, rows, 2):
        xh, xl = split(jnp.concatenate([turned[a], turned[a + 1]], axis=1))
        first = mm(both, xh, NN)
        acc = first[:mu] + first[mu:] + mm(chi, xl, NN)
        tmp[a] = acc[:, :BLOCK]
        tmp[a + 1] = acc[:, BLOCK:]
    out[0] = jnp.transpose(tmp[...], (1, 0, 2)).astype(jnp.bfloat16)


def back_call(coeff, x):
    mu, nocc = coeff.shape
    quarter = x.shape[1]
    rows = 16 if quarter % 16 == 0 else quarter
    return pl.pallas_call(
        back_kernel,
        grid=(quarter // rows,),
        out_shape=jax.ShapeDtypeStruct((1, mu, quarter, BLOCK), jnp.bfloat16),
        in_specs=[pl.BlockSpec((mu, nocc), lambda s: (0, 0)),
                  pl.BlockSpec((nocc, rows, BLOCK), lambda s: (0, s, 0))],
        out_specs=pl.BlockSpec((1, mu, rows, BLOCK), lambda s: (0, 0, s, 0)),
        scratch_shapes=[pltpu.VMEM((rows, mu, BLOCK), jnp.float32)],
        compiler_params=pltpu.CompilerParams(vmem_limit_bytes=40 << 20),
    )(coeff, x)


def shards(geom, three_index, occ_energy, vir_energy, coeff, kept, owner_slot):
    xy, zlen = geom["xy"], geom["z"]
    slots = xy * zlen
    vir, aux = three_index.shape[1], three_index.shape[2]
    block_count = aux // BLOCK
    quarter = vir // 4
    dens, pair_energy, pos, own_at, stab, level = group_call(geom, owner_slot, kept, occ_energy, three_index, vir_energy)

    def plain(dens, stab, pos, own_at, owner_slot):
        matches = owner_slot[None, :] == jnp.arange(slots, dtype=jnp.int32)[:, None]
        slot_block = jnp.sum(jnp.where(matches, jnp.arange(block_count, dtype=jnp.int32)[None, :], 0), axis=1)
        used = jnp.any(matches, axis=1)
        picked = jnp.take(dens.reshape(block_count, 4, quarter, BLOCK), slot_block, axis=0)
        out = jnp.where(used[:, None, None, None], picked, 0.0)
        return lax.all_to_all(out, "occ", split_axis=0, concat_axis=0, tiled=True)

    branches = [plain]
    for n, caps in enumerate(geom["caps"][::-1]):
        branches.append(lambda dens, stab, pos, own_at, owner_slot, caps=caps, n=n: exchange_call(
            geom, caps, n + 1, dens, stab, pos, own_at))
    recv = lax.switch(level[0, 0], branches, dens, stab, pos, own_at, owner_slot)
    return (pair_energy, back_call(coeff, recv.reshape(slots * 4, quarter, BLOCK)))


GEOM = {
    64: {"xy": 8, "z": 8, "chunks": 10, "unit": 4,
         "caps": [(52, 40, 28, 12), (56, 44, 28, 12), (56, 44, 32, 12), (60, 48, 32, 16), (64, 52, 36, 16), (72, 60, 40, 16),
                  (88, 68, 44, 16)]},
}


def solution(mesh):
    in_specs = (P(("occ", "pair"), None, None), P(), P(), P(), P(("occ", "pair"), None), P())
    out_specs = (P(("occ", "pair"), None), P("occ", None, "pair", None))
    return jax.shard_map(functools.partial(shards, GEOM[mesh.shape["occ"]]), mesh=mesh, in_specs=in_specs,
                         out_specs=out_specs, check_vma=False)
```

```python
import functools
import jax
import jax.numpy as jnp
from jax import lax
from jax.experimental import pallas as pl
from jax.experimental.pallas import tpu as pltpu
from jax.sharding import PartitionSpec as P

BLOCK = 128
MESH = pl.DeviceIdType.MESH
NT = (((1,), (1,)), ((), ()))
NN = (((1,), (0,)), ((), ()))


def split(x):
    hi = x.astype(jnp.bfloat16)
    return hi, (x - hi.astype(jnp.float32)).astype(jnp.bfloat16)


def mm(a, b, dims):
    return lax.dot_general(a, b, dims, preferred_element_type=jnp.float32)


def group_kernel(cfg, owner, kept, gen, own, vrow,
                 dens_out, energy_out, pos, own_at, stab, level,
                 ball, gram, sc, vcol, dens, etile, ebuf, lbuf, live, row, cells, best, near, rows_s,
                 loc, s_f, r_f, s_o, r_o, s_p, r_p, s_e, r_e, s_l, r_l, s_d, s_c, r_c, s_x, r_x):
    (xy, zlen, chunks, wide, caps, block_count) = cfg
    hops = zlen // 2
    slots = xy * zlen
    occ = lax.axis_index("occ")
    p = lax.axis_index("pair")
    me = occ // zlen
    z = occ % zlen
    p_far = (p + 2) % 4
    p_sib = p + 1 - 2 * (p % 2)
    sib = (occ, p_sib)
    far = (occ, p_far)
    vir = ball.shape[1]
    quarter = vir // 4
    column = [(a, b) for a in range(zlen) for b in range(4) if (a, b) != (0, 0)]

    def mate(a, b):
        return (occ - z + (z + a) % zlen, (p + b) % 4)

    def cell(d):
        return ((me + d) % xy * zlen + z, p)

    def remote(src, dst, ss, rs, dev):
        return pltpu.make_async_remote_copy(src_ref=src, dst_ref=dst, send_sem=ss, recv_sem=rs,
                                            device_id=dev, device_id_type=MESH)

    def loop(n, f):
        lax.fori_loop(0, n, lambda k, c: (f(k), c)[1], 0)

    def cols(k):
        return pl.ds(pl.multiple_of(k * wide, 128), wide)

    def c_local(k):
        return pltpu.make_async_copy(own.at[0, :, cols(k)], ball.at[p, :, cols(k)], loc.at[k])

    barrier = pltpu.get_barrier_semaphore()
    greet = [mate(a, b) for a, b in column] + [cell(d) for d in range(1, xy)]
    for dev in greet:
        pl.semaphore_signal(barrier, inc=1, device_id=dev, device_id_type=MESH)
    loop(chunks, lambda k: c_local(k).start())

    lane = lax.broadcasted_iota(jnp.int32, (8, 128), 1)
    slot = lane % slots
    block = jnp.full((8, 128), -1, jnp.int32)
    for c in range(block_count):
        block = jnp.where(slot == owner[c], c, block)
    have = jnp.zeros((8, 128), jnp.int32)
    alive = jnp.zeros((8, 128), jnp.int32)
    for k in range(kept.shape[1]):
        have = jnp.where(block == kept[0, k], 1, have)
        alive = jnp.where(lane == kept[0, k], 1, alive)
    row[...] = have
    live[...] = alive.astype(jnp.float32)
    lbuf[0] = live[...]
    vcol[...] = jnp.transpose(jnp.broadcast_to(vrow[...], (128, vir)))
    pl.semaphore_wait(barrier, len(greet))

    def c_far(k):
        return remote(ball.at[p, :, cols(k)], ball.at[p, :, cols(k)], s_f.at[k], r_f.at[k], far)

    def a_far(k):
        return remote(ball.at[p, :, cols(k)], ball.at[p_far, :, cols(k)], s_f.at[k], r_f.at[k], far)

    def c_sib_own(k):
        return remote(ball.at[p, :, cols(k)], ball.at[p, :, cols(k)], s_o.at[k], r_o.at[k], sib)

    def a_sib_own(k):
        return remote(ball.at[p, :, cols(k)], ball.at[p_sib, :, cols(k)], s_o.at[k], r_o.at[k], sib)

    def c_sib_far(k):
        return remote(ball.at[p_far, :, cols(k)], ball.at[p_far, :, cols(k)], s_p.at[k], r_p.at[k], sib)

    p_sibfar = (p_sib + 2) % 4

    def a_sib_far(k):
        return remote(ball.at[p_far, :, cols(k)], ball.at[p_sibfar, :, cols(k)], s_p.at[k], r_p.at[k], sib)

    def c_live(d):
        return remote(live, lbuf.at[d], s_l.at[d - 1], r_l.at[d - 1], (occ, (p + d) % 4))

    def c_row(n, a, b):
        return pltpu.make_async_remote_copy(src_ref=row, dst_ref=cells.at[z, p], send_sem=s_c.at[n], recv_sem=r_c.at[a, b],
                                            device_id=mate(a, b), device_id_type=MESH)

    def a_row(n, a, b):
        return pltpu.make_async_remote_copy(src_ref=row, dst_ref=cells.at[(z + zlen - a) % zlen, (p + 4 - b) % 4],
                                            send_sem=s_c.at[n], recv_sem=r_c.at[a, b],
                                            device_id=mate(a, b), device_id_type=MESH)

    def send_own(k):
        c_local(k).wait()
        c_far(k).start()
        c_sib_own(k).start()

    send_own(0)
    for n, (a, b) in enumerate(column):
        c_row(n, a, b).start()
    for d in (1, 2, 3):
        c_live(d).start()
    loop(chunks - 1, lambda k: send_own(k + 1))
    cells[z, p] = row[...]
    gram[...] = jnp.zeros_like(gram)
    for n, (a, b) in enumerate(column):
        a_row(n, a, b).wait_recv()
    source = lax.broadcasted_iota(jnp.int32, (8, 128), 0)
    dest = slot % zlen
    order = slot // zlen
    flag = []
    for i in range(4):
        f = jnp.zeros((8, 128), jnp.int32)
        for a in range(zlen):
            f = jnp.where(source == a, cells[a, i], f)
        flag.append(f)
        own_at[i] = jnp.where(f > 0, block * 4 + i, -1)

    roll = lambda v, n: pltpu.roll(v, n % 128, 1)
    needs = [jnp.zeros((8, 128), jnp.int32) for _ in range(hops)]
    for side, sign in enumerate((1, -1)):
        dist = (sign * (dest - source) + 2 * zlen) % zlen
        xs = []
        for i in range(4):
            tie = (i < 2) == (sign == 1)
            ok = (dist >= 1) & (dist <= (hops if tie else hops - 1))
            xs.append(jnp.where(ok, flag[i], 0))
        totals, before = [], []
        for x in xs:
            t, e, n = x, x, 1
            while n < xy:
                t = t + roll(t, n * zlen)
                e = e + jnp.where(order >= n, roll(e, n * zlen), 0)
                n *= 2
            totals.append(t)
            before.append(e - x)
        total = totals[0] + totals[1] + totals[2] + totals[3]
        farther = jnp.zeros((8, 128), jnp.int32)
        for k in range(1, hops):
            farther = farther + jnp.where(dist + k <= hops, roll(total, -sign * k), 0)
        upto = farther
        for i in range(4):
            pos[side, i] = jnp.where(xs[i] > 0, upto + before[i], -1)
            upto = upto + totals[i]
        for h in range(1, hops + 1):
            needs[h - 1] = jnp.maximum(needs[h - 1], jnp.where(dist == h, farther + total, 0))

    need_tile = jnp.zeros((8, 128), jnp.float32)
    for h in range(hops):
        need_tile = need_tile + jnp.where(lane == h, jnp.max(needs[h].astype(jnp.float32)), 0.0)
    best[...] = need_tile

    at = lax.broadcasted_iota(jnp.int32, (128, 128), 1).astype(jnp.float32)
    inside = lax.broadcasted_iota(jnp.int32, (128, 128), 0) < slots
    tall = lambda v: jnp.transpose(jnp.broadcast_to(v.astype(jnp.float32), (128, 128)))
    rows_s[...] = block
    what = tall(rows_s[0:1, :] * 4)
    for side in range(2):
        acc = jnp.zeros((128, 128), jnp.float32)
        for i in range(4):
            where = tall(pos[side, i, pl.ds(z, 1), :])
            acc = acc + jnp.where((where == at) & inside, what + float(i), 0.0)
        stab[side] = jnp.broadcast_to(jnp.sum(acc, axis=0, keepdims=True), (8, 128)).astype(jnp.int32)


    def c_best(d):
        return remote(best, near.at[d - 1], s_x.at[d - 1], r_x.at[d - 1], cell(d))

    for d in range(1, xy):
        c_best(d).start()

    def pass_on(k):
        a_far(k).wait_recv()
        c_sib_far(k).start()

    def gram_chunk(k):
        a_sib_own(k).wait_recv()
        a_sib_far(k).wait_recv()
        mine = jnp.concatenate(
            [ball[i, pl.ds(pl.multiple_of(p * quarter, quarter), quarter), cols(k)] for i in range(4)], axis=0)
        hi, low = split(mine)
        both = jnp.concatenate([hi, low], axis=0)
        for j in range(4):
            bh, bl = split(ball[j, :, cols(k)])
            first = mm(both, bh, NT)
            gram[:, j * vir:(j + 1) * vir] += first[:vir] + first[vir:] + mm(hi, bl, NT)

    pass_on(0)

    def step(k):
        pass_on(k + 1)
        gram_chunk(k)

    loop(chunks - 1, step)
    gram_chunk(chunks - 1)

    band = lax.broadcasted_iota(jnp.int32, (8, 128), 0)
    va = vcol[pl.ds(pl.multiple_of(p * quarter, quarter), quarter), 0:1]
    vb = vrow[0:1, :]
    tile = jnp.zeros((8, 128), jnp.float32)
    for i in range(4):
        for j in range(4):
            g = gram[i * quarter:(i + 1) * quarter, j * vir:(j + 1) * vir]
            t = gram[j * quarter:(j + 1) * quarter, i * vir:(i + 1) * vir]
            x = (2.0 * g - t) / (gen[occ * 4 + i] + gen[occ * 4 + j] - va - vb)
            hi, low = split(x)
            sc[i * quarter:(i + 1) * quarter, j * vir:(j + 1) * vir] = hi
            sc[vir + i * quarter:vir + (i + 1) * quarter, j * vir:(j + 1) * vir] = low
            tile = tile + jnp.where((band == i) & (lane == j), jnp.sum(g * x), 0.0)
    etile[...] = tile

    for d in (1, 2, 3):
        c_live(d).wait()
    live_of = []
    for i in range(4):
        v = jnp.zeros((8, 128), jnp.float32)
        for d in range(4):
            v = v + jnp.where((p + 4 - d) % 4 == i, lbuf[d], 0.0)
        live_of.append(v)

    def c_energy(d):
        return remote(etile, ebuf.at[d - 1], s_e.at[d - 1], r_e.at[d - 1], (occ, (p + d) % 4))

    for d in (1, 2, 3):
        c_energy(d).start()

    def c_dens(k):
        return pltpu.make_async_copy(dens.at[pl.ds(k * 8, 8)], dens_out.at[pl.ds(k * 8, 8)], s_d.at[k])

    def density(k):
        cc = pl.ds(pl.multiple_of(k * 2 * BLOCK, 256), 2 * BLOCK)
        bh, bl = split(ball[:, :, cc].reshape(4 * vir, 2 * BLOCK))
        first = mm(sc[...], bh, NN)
        acc = first[:vir] + first[vir:] + mm(sc[0:vir], bl, NN)
        for h in range(2):
            for i in range(4):
                w = jnp.sum(jnp.where(lane == 2 * k + h, live_of[i], 0.0), axis=1, keepdims=True)[0:1]
                dens[(2 * k + h) * 4 + i] = acc[i * quarter:(i + 1) * quarter, h * BLOCK:(h + 1) * BLOCK] * w

    steps = block_count // 2
    density(0)

    def dense(k):
        density(k + 1)
        c_dens(k).start()

    loop(steps - 1, dense)

    for d in range(1, xy):
        c_best(d).wait()
    most = best[...]
    for d in range(xy - 1):
        most = jnp.maximum(most, near[d])
    fits = jnp.zeros((8, 128), jnp.int32)
    for cap in caps:
        over = jnp.zeros((8, 128), jnp.float32)
        for h in range(hops):
            over = over + jnp.where((lane == h) & (most > float(cap[h])), 1.0, 0.0)
        fits = fits + jnp.where(jnp.max(over) > 0.0, 0, 1)
    level[...] = fits
    for n, (a, b) in enumerate(column):
        c_row(n, a, b).wait_send()


    c_dens(steps - 1).start()
    for d in (1, 2, 3):
        c_energy(d).wait()
    etile[...] = etile[...] + (ebuf[0] + (ebuf[1] + ebuf[2]))
    energy_out[...] = etile[pl.ds(p, 1), 0:4]

    def drain(k):
        c_far(k).wait_send()
        c_sib_own(k).wait_send()
        c_sib_far(k).wait_send()

    loop(chunks, drain)
    loop(steps, lambda k: c_dens(k).wait())


def group_call(geom, owner_slot, kept, occ_energy, three_index, vir_energy):
    vir, aux = three_index.shape[1], three_index.shape[2]
    xy, zlen, chunks = geom["xy"], geom["z"], geom["chunks"]
    wide = aux // chunks
    quarter = vir // 4
    blocks = aux // BLOCK
    i32, f32 = jnp.int32, jnp.float32
    dma = lambda *s: pltpu.SemaphoreType.DMA(s)
    vm = pl.BlockSpec(memory_space=pltpu.VMEM)
    sm = pl.BlockSpec(memory_space=pltpu.SMEM)
    hb = pl.BlockSpec(memory_space=pl.ANY)
    sd = jax.ShapeDtypeStruct
    tile = (8, 128)
    return pl.pallas_call(
        functools.partial(group_kernel, (xy, zlen, chunks, wide, geom["caps"], blocks)),
        out_shape=(sd((4 * blocks, quarter, BLOCK), f32), sd((1, 4), f32), sd((2, 4) + tile, i32), sd((4,) + tile, i32),
                   sd((2,) + tile, i32), sd(tile, i32)),
        in_specs=[sm, sm, sm, hb, vm],
        out_specs=(hb, vm, vm, vm, vm, vm),
        scratch_shapes=[
            pltpu.VMEM((4, vir, aux), f32),
            pltpu.VMEM((vir, 4 * vir), f32),
            pltpu.VMEM((2 * vir, 4 * vir), jnp.bfloat16),
            pltpu.VMEM((vir, 128), f32),
            pltpu.VMEM((4 * blocks, quarter, BLOCK), f32),
            pltpu.VMEM(tile, f32),
            pltpu.VMEM((3,) + tile, f32),
            pltpu.VMEM((4,) + tile, f32),
            pltpu.VMEM(tile, f32),
            pltpu.VMEM(tile, i32),
            pltpu.VMEM((zlen, 4) + tile, i32),
            pltpu.VMEM(tile, f32),
            pltpu.VMEM((xy - 1,) + tile, f32),
            pltpu.VMEM(tile, i32),
        ] + [dma(chunks)] * 7 + [dma(3)] * 4 + [dma(blocks // 2), dma(4 * zlen - 1), dma(zlen, 4), dma(xy - 1), dma(xy - 1)],
        compiler_params=pltpu.CompilerParams(collective_id=0, has_side_effects=True, vmem_limit_bytes=58 << 20),
    )(owner_slot, kept, occ_energy, three_index, vir_energy.reshape(1, vir))


def exchange_kernel(cfg, stab, pos, own_at, dens_in, recv, dens, zsend, xs, *refs):
    (xy, zlen, caps, unit) = cfg
    hops = zlen // 2
    rounds = zsend.shape[0]
    rows = zsend.shape[3]
    refs = list(refs)
    take = lambda n: [refs.pop(0) for _ in range(n)]
    keys = [(rd, sign, h) for rd in range(rounds) for sign in (1, -1) for h in range(hops)]
    arr = dict(zip(keys, take(len(keys))))
    zss = dict(zip(keys, take(len(keys))))
    zrs = dict(zip(keys, take(len(keys))))
    xs_s, xs_r, xs_l, s_in = take(4)
    occ = lax.axis_index("occ")
    p = lax.axis_index("pair")
    me = occ // zlen
    z = occ % zlen
    to = {1: (occ - z + (z + 1) % zlen, p), -1: (occ - z + (z + zlen - 1) % zlen, p)}
    side = {1: 0, -1: 1}

    def cell(d):
        return ((me + d) % xy * zlen + z, p)

    def remote(src, dst, ss, rs, dev):
        return pltpu.make_async_remote_copy(src_ref=src, dst_ref=dst, send_sem=ss, recv_sem=rs,
                                            device_id=dev, device_id_type=MESH)

    def loop(n, f):
        lax.fori_loop(0, n, lambda k, c: (f(k), c)[1], 0)

    load = pltpu.make_async_copy(dens_in, dens, s_in)
    load.start()
    greet = [to[1], to[-1]] + [cell(d) for d in range(1, xy)]
    barrier = pltpu.get_barrier_semaphore()
    for dev in greet:
        pl.semaphore_signal(barrier, inc=1, device_id=dev, device_id_type=MESH)
    pl.semaphore_wait(barrier, len(greet))
    load.wait()

    def part(rd):
        return pl.ds(rd * rows, rows)

    def c_z(rd, sign, h, k):
        src = zsend.at[rd, side[sign]] if h == 0 else arr[rd, sign, h - 1]
        ks = pl.ds(k * unit, unit)
        return remote(src.at[ks], arr[rd, sign, h].at[ks], zss[rd, sign, h].at[k], zrs[rd, sign, h].at[k], to[sign])

    def own(rd):
        def fill(k):
            for sign in (1, -1):
                for u in range(unit):
                    t = k * unit + u
                    zsend[rd, side[sign], t] = dens[stab[side[sign], 0, t], part(rd)]

        def send(k):
            c_z(rd, 1, 0, k).start()
            c_z(rd, -1, 0, k).start()

        fill(0)

        def first(k):
            fill(k + 1)
            send(k)

        loop(caps[0] // unit - 1, first)
        send(caps[0] // unit - 1)

    per = 2 * hops

    def gpos(d):
        return (me + d) % xy

    def c_xy(rd, r, d, zsrc):
        n = (rd * per + r) * xy + d
        return remote(xs.at[rd, r, gpos(d)], recv.at[me * zlen + zsrc, :, part(rd)], xs_s.at[n], xs_r.at[n], cell(d))

    def a_xy(rd, r, d, zsrc):
        n = (rd * per + r) * xy + d
        return remote(xs.at[rd, r, gpos(d)], recv.at[gpos(xy - d) * zlen + zsrc, :, part(rd)], xs_s.at[n], xs_r.at[n],
                      cell(d))

    def c_self(rd, r, zsrc):
        return pltpu.make_async_copy(xs.at[rd, r, me], recv.at[me * zlen + zsrc, :, part(rd)], xs_l.at[rd * per + r])

    def place(rd, r, table, buf, which, cut):
        def one(j):
            for i in which:
                idx = table(i, j * zlen + z)
                at = jnp.maximum(idx, 0)
                v = buf[at, part(rd)] if cut else buf[at]
                xs[rd, r, j, i] = jnp.where(idx >= 0, v, 0.0)
        loop(xy, one)

    def stood(sign, zsrc):
        return lambda i, s: pos[side[sign], i, zsrc, s]

    done = []

    def deliver(rd, r, zsrc):
        loop(xy - 1, lambda d: c_xy(rd, r, d + 1, zsrc).start())
        c_self(rd, r, zsrc).start()
        done.append((rd, r, zsrc))

    def hop(rd, h):
        def forward(k):
            for sign in (1, -1):
                c_z(rd, sign, h - 1, k).wait_recv()
                if h < hops:
                    @pl.when(k < caps[h] // unit)
                    def _(sign=sign):
                        c_z(rd, sign, h, k).start()
        loop(caps[h - 1] // unit, forward)

    def settle(rd, h):
        if h < hops:
            for n, sign in enumerate((1, -1)):
                r = 1 + 2 * (h - 1) + n
                zsrc = (z + zlen - sign * h) % zlen
                place(rd, r, stood(sign, zsrc), arr[rd, sign, h - 1], range(4), False)
                deliver(rd, r, zsrc)
        else:
            r = 2 * hops - 1
            zsrc = (z + h) % zlen
            place(rd, r, stood(1, zsrc), arr[rd, 1, h - 1], (0, 1), False)
            place(rd, r, stood(-1, zsrc), arr[rd, -1, h - 1], (2, 3), False)
            deliver(rd, r, zsrc)

    own(0)
    for rd in range(rounds):
        place(rd, 0, lambda i, s: own_at[i, z, s], dens, range(4), True)
        deliver(rd, 0, z)
    hop(0, 1)
    settle(0, 1)
    hop(0, 2)
    settle(0, 2)
    hop(0, 3)
    own(1)
    settle(0, 3)
    hop(0, 4)
    settle(0, 4)
    hop(1, 1)
    settle(1, 1)
    for h in (2, 3, 4):
        hop(1, h)
        settle(1, h)

    for rd, r, zsrc in done:
        c_self(rd, r, zsrc).wait()

        def finish(d, rd=rd, r=r, zsrc=zsrc):
            a_xy(rd, r, d + 1, zsrc).wait_recv()
            c_xy(rd, r, d + 1, zsrc).wait_send()
        loop(xy - 1, finish)
    for rd, sign, h in keys:
        loop(caps[h] // unit, lambda k, rd=rd, sign=sign, h=h: c_z(rd, sign, h, k).wait_send())


def exchange_call(geom, caps, ident, dens, stab, pos, own_at):
    xy, zlen, unit = geom["xy"], geom["z"], geom["unit"]
    hops = zlen // 2
    rounds = 2
    quarter = dens.shape[1]
    rows = quarter // rounds
    f32 = jnp.float32
    dma = lambda *s: pltpu.SemaphoreType.DMA(s)
    sm = pl.BlockSpec(memory_space=pltpu.SMEM)
    hb = pl.BlockSpec(memory_space=pl.ANY)
    piece = (rows, BLOCK)
    order = [caps[h] for rd in range(rounds) for sign in (1, -1) for h in range(hops)]
    n = rounds * 2 * hops
    return pl.pallas_call(
        functools.partial(exchange_kernel, (xy, zlen, caps, unit)),
        out_shape=jax.ShapeDtypeStruct((xy * zlen, 4, quarter, BLOCK), f32),
        in_specs=[sm, sm, sm, hb],
        out_specs=hb,
        scratch_shapes=[pltpu.VMEM(dens.shape, f32), pltpu.VMEM((rounds, 2, caps[0]) + piece, f32),
                        pltpu.VMEM((rounds, 2 * hops, xy, 4) + piece, f32)]
        + [pltpu.VMEM((c,) + piece, f32) for c in order] + [dma(c // unit) for c in order] * 2
        + [dma(n * xy), dma(n * xy), dma(n), pltpu.SemaphoreType.DMA],
        compiler_params=pltpu.CompilerParams(collective_id=ident, has_side_effects=True, vmem_limit_bytes=58 << 20),
    )(stab, pos, own_at, dens)


def back_kernel(coeff, x, out, tmp):
    chi, clo = split(coeff[...])
    both = jnp.concatenate([chi, clo], axis=0)
    mu = coeff.shape[0]
    rows = x.shape[1]
    turned = jnp.transpose(x[...], (1, 0, 2))
    for a in range(0, rows, 2):
        xh, xl = split(jnp.concatenate([turned[a], turned[a + 1]], axis=1))
        first = mm(both, xh, NN)
        acc = first[:mu] + first[mu:] + mm(chi, xl, NN)
        tmp[a] = acc[:, :BLOCK]
        tmp[a + 1] = acc[:, BLOCK:]
    out[0] = jnp.transpose(tmp[...], (1, 0, 2)).astype(jnp.bfloat16)


def back_call(coeff, x):
    mu, nocc = coeff.shape
    quarter = x.shape[1]
    rows = 16 if quarter % 16 == 0 else quarter
    return pl.pallas_call(
        back_kernel,
        grid=(quarter // rows,),
        out_shape=jax.ShapeDtypeStruct((1, mu, quarter, BLOCK), jnp.bfloat16),
        in_specs=[pl.BlockSpec((mu, nocc), lambda s: (0, 0)),
                  pl.BlockSpec((nocc, rows, BLOCK), lambda s: (0, s, 0))],
        out_specs=pl.BlockSpec((1, mu, rows, BLOCK), lambda s: (0, 0, s, 0)),
        scratch_shapes=[pltpu.VMEM((rows, mu, BLOCK), jnp.float32)],
        compiler_params=pltpu.CompilerParams(vmem_limit_bytes=40 << 20),
    )(coeff, x)


def shards(geom, three_index, occ_energy, vir_energy, coeff, kept, owner_slot):
    xy, zlen = geom["xy"], geom["z"]
    slots = xy * zlen
    vir, aux = three_index.shape[1], three_index.shape[2]
    block_count = aux // BLOCK
    quarter = vir // 4
    dens, pair_energy, pos, own_at, stab, level = group_call(geom, owner_slot, kept, occ_energy, three_index, vir_energy)

    def plain(dens, stab, pos, own_at, owner_slot):
        matches = owner_slot[None, :] == jnp.arange(slots, dtype=jnp.int32)[:, None]
        slot_block = jnp.sum(jnp.where(matches, jnp.arange(block_count, dtype=jnp.int32)[None, :], 0), axis=1)
        used = jnp.any(matches, axis=1)
        picked = jnp.take(dens.reshape(block_count, 4, quarter, BLOCK), slot_block, axis=0)
        out = jnp.where(used[:, None, None, None], picked, 0.0)
        return lax.all_to_all(out, "occ", split_axis=0, concat_axis=0, tiled=True)

    branches = [plain]
    for n, caps in enumerate(geom["caps"][::-1]):
        branches.append(lambda dens, stab, pos, own_at, owner_slot, caps=caps, n=n: exchange_call(
            geom, caps, n + 1, dens, stab, pos, own_at))
    recv = lax.switch(level[0, 0], branches, dens, stab, pos, own_at, owner_slot)
    return (pair_energy, back_call(coeff, recv.reshape(slots * 4, quarter, BLOCK)))


GEOM = {
    64: {"xy": 8, "z": 8, "chunks": 10, "unit": 4,
         "caps": [(52, 40, 28, 12), (56, 44, 28, 12), (56, 44, 32, 12), (60, 48, 32, 16), (64, 52, 36, 16), (72, 60, 40, 16),
                  (88, 68, 44, 16)]},
}


def solution(mesh):
    in_specs = (P(("occ", "pair"), None, None), P(), P(), P(), P(("occ", "pair"), None), P())
    out_specs = (P(("occ", "pair"), None), P("occ", None, "pair", None))
    return jax.shard_map(functools.partial(shards, GEOM[mesh.shape["occ"]]), mesh=mesh, in_specs=in_specs,
                         out_specs=out_specs, check_vma=False)
```
